32 devices in a mesh: lines: 8 (over z, x), temp: 4 (over y, core).
Axes of the slice: x: 2, y: 2, z: 4, core: 2. Of those that a mesh axis runs over, the one named last changes fastest.
Arguments:
- line_position: float32 [384, 128], P('lines'), may hold values from 0 to 256
- line_strength: float32 [384, 128], P('lines'), may hold values from 0.05 to 1
- lower_energy: float32 [384, 128], P('lines'), may hold values from 0 to 1500
- broad_width: float32 [384, 128], P('lines'), may hold values from 0.3 to 3
- broad_exponent: float32 [384, 128], P('lines'), may hold values from 0.3 to 1
- doppler_width: float32 [384, 128], P('lines'), may hold values from 0.3 to 3
- block_window: int32 [384], P('lines'), may hold values from 0 to 31, as said below
- tile_offset: int32 [384], P('lines'), may hold values from 0 to 1792
- owner_slot: int32 [32], replicated, may hold values from 0 to 31, as said below
Outputs:
- polynomial_weights: float32 [8, 32, 2048], P('temp', 'lines')
The draws below stay inside these ranges and needn't reach their ends.
Inputs may be any that keep to these rules, and one draw needn't show every extreme that they name: owner_slot is a permutation of the 32 window places. `block_window`: of the 48 blocks of one index of lines, exactly 12 fall on windows of each of 2 owners and 4 on windows of each other owner; some owner receives 12 blocks from every index of lines.
All inputs are finite; a program needn't handle non-finite values.
Results may differ from the reference program's by a relative error of at most 0.00015.
Values sent between devices are 32-bit elements; how exact they have to be, the bound alone decides.
No kernel may reach another device: no remote copies, remote signals or barrier semaphores. Data moves between devices by JAX's collectives and lax.ppermute only.
A program may use at most 128 MiB of HBM per device.

```python
import math
import jax
import jax.numpy as jnp
from jax import lax

LINES_BLK = 128
PATCH_SAMPLES = 256
SPAN_SAMPLES = 2048
THERMAL_SAMPLES = 8
BLK_DEV = 48
WIN_DEV = 4
BLOCKS = 384
SPECTRAL_SPANS = 32
N_LINES = 8


def routing_tables(key):
    owner_slot = jax.random.permutation(jax.random.fold_in(key, 11), SPECTRAL_SPANS).astype(jnp.int32)
    unit = 2 * BLK_DEV // (3 * N_LINES)
    quarter = N_LINES // 4
    half_blocks = BLK_DEV // 2
    order = jnp.arange(BLK_DEV, dtype=jnp.int32)
    owner_rank = jnp.where(order < half_blocks, order // (3 * unit), quarter + (order - half_blocks) // unit)
    base_order = jax.random.permutation(jax.random.fold_in(key, 12), N_LINES).astype(jnp.int32)
    shifts = jax.random.randint(jax.random.fold_in(key, 13), (N_LINES,), 0, quarter)
    owner_index = base_order[(owner_rank[None, :] - shifts[:, None]) % N_LINES]
    local_window = jax.random.randint(jax.random.fold_in(key, 14), (N_LINES, BLK_DEV), 0, WIN_DEV)
    slot_index = owner_index * WIN_DEV + local_window
    inverse = jnp.zeros((SPECTRAL_SPANS,), jnp.int32).at[owner_slot].set(jnp.arange(SPECTRAL_SPANS, dtype=jnp.int32))
    window_of = inverse[slot_index]
    shuffle_keys = jax.random.split(jax.random.fold_in(key, 15), N_LINES)
    shuffles = jax.vmap(lambda one_key: jax.random.permutation(one_key, BLK_DEV))(shuffle_keys)
    window_of = jnp.take_along_axis(window_of, shuffles, axis=1)
    return (owner_slot, window_of.reshape(-1).astype(jnp.int32))


def draw_owner_slot(key, part):
    return routing_tables(key)[0]


def draw_block_window(key, part):
    return routing_tables(key)[1]


def plant(drawn, key, least, top_value):
    spot = [jax.random.randint(jax.random.fold_in(key, axis), (), 0, length) for axis, length in enumerate(drawn.shape)]
    main_axis = drawn.shape.index(max(drawn.shape))
    neighbour = spot[:main_axis] + [(spot[main_axis] + 1) % drawn.shape[main_axis]] + spot[main_axis + 1:]
    return drawn.at[tuple(spot)].set(least).at[tuple(neighbour)].set(top_value)


def levels(own_key, dims, cuts, low, largest):
    def one(position, blocks):
        draws = jax.random.uniform(jax.random.fold_in(jax.random.fold_in(own_key, 6), position), (blocks,), jnp.float32, low / len(cuts), largest / len(cuts))
        return jnp.repeat(jnp.exp(draws), dims[position] // blocks).reshape((-1,) + (1,) * (len(dims) - position - 1))

    gain = one(*cuts[0])
    for cut in cuts[1:]:
        gain = gain * one(*cut)
    return gain


def setup_inputs(seed: int = 0) -> dict:
    key_of = jax.random.split(jax.random.key(seed), 10)
    return {
        "line_position": jnp.clip(256.0 * jax.random.uniform(key_of[0], (BLOCKS, LINES_BLK), jnp.float32) ** levels(key_of[0], (BLOCKS, LINES_BLK), ((0, 8),), -0.2, 0.2), 0.0, 256.0),
        "line_strength": jnp.clip(jnp.exp(math.log(1.0) - 2.9957323 * jax.random.uniform(key_of[1], (BLOCKS, LINES_BLK), jnp.float32) ** levels(key_of[1], (BLOCKS, LINES_BLK), ((0, 8),), -0.2, 0.2)), 0.05, 1.0),
        "lower_energy": jnp.clip(1500.0 * jax.random.uniform(key_of[2], (BLOCKS, LINES_BLK), jnp.float32) ** levels(key_of[2], (BLOCKS, LINES_BLK), ((0, 8),), -0.2, 0.2), 0.0, 1500.0),
        "broad_width": jnp.clip(jnp.exp(math.log(3.0) - 2.3025851 * jax.random.uniform(key_of[3], (BLOCKS, LINES_BLK), jnp.float32) ** levels(key_of[3], (BLOCKS, LINES_BLK), ((0, 8),), -0.2, 0.2)), 0.3, 3.0),
        "broad_exponent": jnp.clip(0.3 + 0.7 * jax.random.uniform(key_of[4], (BLOCKS, LINES_BLK), jnp.float32) ** levels(key_of[4], (BLOCKS, LINES_BLK), ((0, 8),), -0.2, 0.2), 0.3, 1.0),
        "doppler_width": jnp.clip(jnp.exp(math.log(3.0) - 2.3025851 * jax.random.uniform(key_of[5], (BLOCKS, LINES_BLK), jnp.float32) ** levels(key_of[5], (BLOCKS, LINES_BLK), ((0, 8),), -0.2, 0.2)), 0.3, 3.0),
        "block_window": draw_block_window(jax.random.fold_in(key_of[9], 71), 0),
        "tile_offset": plant(jax.random.randint(key_of[7], (BLOCKS,), 0, SPAN_SAMPLES - PATCH_SAMPLES + 1), jax.random.fold_in(key_of[7], 1), 0, SPAN_SAMPLES - PATCH_SAMPLES).astype(jnp.int32),
        "owner_slot": draw_owner_slot(jax.random.fold_in(key_of[9], 71), 0),
    }


REFERENCE_KELVIN = 1000.0

def thermal_abscissae(line_count):
    theta = math.pi * (jnp.arange(line_count, dtype=jnp.float32) + 0.5) / line_count
    return 1650.0 + 1350.0 * jnp.cos(theta)

def polynomial_regression(line_count):
    order = jnp.arange(line_count, dtype=jnp.float32)
    theta = math.pi * (jnp.arange(line_count, dtype=jnp.float32) + 0.5) / line_count
    factor = jnp.where(order == 0.0, 1.0 / line_count, 2.0 / line_count)
    return factor[:, None] * jnp.cos(order[:, None] * theta[None, :])

def shape_function_piece(transition_position, base_intensity, lower_level_term, collisional_broadening_base, collisional_power_law, thermal_broadening_scale, kelvin_value, wavenumber_points):
    reciprocal_kelvin = 1.0 / kelvin_value
    temp_ratio = REFERENCE_KELVIN * reciprocal_kelvin
    scaled = base_intensity * jnp.exp(-lower_level_term * (reciprocal_kelvin - 1.0 / REFERENCE_KELVIN))
    lorentz_width = 2.0 * collisional_broadening_base * jnp.exp(collisional_power_law * jnp.log(temp_ratio))
    gaussian_halfwidth = 2.35482 * thermal_broadening_scale * jnp.sqrt(kelvin_value / REFERENCE_KELVIN)
    gw, lw = (gaussian_halfwidth, lorentz_width)
    full_width = (gw ** 5 + 2.69269 * gw ** 4 * lw + 2.42843 * gw ** 3 * lw ** 2 + 4.47163 * gw ** 2 * lw ** 3 + 0.07842 * gw * lw ** 4 + lw ** 5) ** 0.2
    share = lw / full_width
    mixing = 1.36603 * share - 0.47719 * share ** 2 + 0.11116 * share ** 3
    grid_points = jnp.arange(wavenumber_points, dtype=jnp.float32) + 0.5
    distance = grid_points - transition_position[..., None]
    half_width = 0.5 * full_width[..., None]
    lorentz = half_width / (math.pi * (distance * distance + half_width * half_width))
    wide = full_width[..., None]
    gaussian = 0.939437 / wide * jnp.exp(-2.7725887 * distance * distance / (wide * wide))
    mixed = mixing[..., None]
    return lax.optimization_barrier(jnp.sum(scaled[..., None] * (mixed * lorentz + (1.0 - mixed) * gaussian), axis=-2))

def reference(line_position, line_strength, lower_energy, broad_width, broad_exponent, doppler_width, block_window, tile_offset, owner_slot):
    thermal_readings = thermal_abscissae(THERMAL_SAMPLES)
    slot_index = owner_slot[block_window].astype(jnp.int32)
    begin = (slot_index * SPAN_SAMPLES + tile_offset).astype(jnp.int32)
    group_size = BLK_DEV // 24
    line_count = BLOCKS // group_size
    argument_bundle = tuple((a.reshape(line_count, group_size, LINES_BLK) for a in (line_position, line_strength, lower_energy, broad_width, broad_exponent, doppler_width)))
    argument_bundle = argument_bundle + (begin.reshape(line_count, group_size),)
    tile_span = jnp.arange(PATCH_SAMPLES, dtype=jnp.int32)

    def accumulate_cohort(absorption_curves, pieces):
        transition_position, base_intensity, lower_level_term, collisional_broadening_base, collisional_power_law, thermal_broadening_scale, starts = pieces
        patch_entries = jnp.stack([shape_function_piece(transition_position, base_intensity, lower_level_term, collisional_broadening_base, collisional_power_law, thermal_broadening_scale, thermal_readings[thermal_position], PATCH_SAMPLES) for thermal_position in range(THERMAL_SAMPLES)])
        flat_index = starts[:, None] + tile_span[None, :]
        return (absorption_curves.at[:, flat_index].add(patch_entries), None)
    absorption_curves, unused_item = lax.scan(accumulate_cohort, jnp.zeros((THERMAL_SAMPLES, SPECTRAL_SPANS * SPAN_SAMPLES), jnp.float32), argument_bundle)
    regression_matrix = polynomial_regression(THERMAL_SAMPLES)
    polynomial_weights = jnp.dot(regression_matrix, absorption_curves, precision=lax.Precision.HIGHEST, preferred_element_type=jnp.float32)
    return polynomial_weights.reshape(THERMAL_SAMPLES, SPECTRAL_SPANS, SPAN_SAMPLES)
```

```python
import functools
import math

import jax
import jax.numpy as jnp
import numpy as np
from jax import lax
from jax.experimental import pallas as pl
from jax.experimental.pallas import tpu as pltpu
from jax.sharding import PartitionSpec as P

LANES = 128
ROWS = 8
PATCH_SAMPLES = 256
SPAN_SAMPLES = 2048
THERMAL_SAMPLES = 8
REFERENCE_KELVIN = 1000.0
PACK = 4
PIECE = LANES // PACK
SEATS = 16
HIGHEST = lax.Precision.HIGHEST


def kelvins():
    theta = math.pi * (np.arange(THERMAL_SAMPLES) + 0.5) / THERMAL_SAMPLES
    return [float(k) for k in 1650.0 + 1350.0 * np.cos(theta)]


def regression():
    order = np.arange(THERMAL_SAMPLES)
    theta = math.pi * (np.arange(THERMAL_SAMPLES) + 0.5) / THERMAL_SAMPLES
    factor = np.where(order == 0, 1.0, 2.0) / THERMAL_SAMPLES
    return factor[:, None] * np.cos(order[:, None] * theta[None, :])


class Plan:
    def __init__(self, lines_n, temp_n, blocks, spans):
        self.lines_n, self.temp_n, self.blocks, self.spans = lines_n, temp_n, blocks, spans
        self.held = spans // lines_n
        self.orders = THERMAL_SAMPLES // temp_n
        self.share = -(-blocks // temp_n)
        self.quads = -(-self.share // PACK)
        heavy = 3 * ((2 * blocks) // (3 * lines_n))
        self.cap = -(-heavy // temp_n)
        self.data_rows = self.cap * self.orders
        self.rows = -(-(self.data_rows + (self.cap + 1) // 2) // ROWS) * ROWS
        self.depth = THERMAL_SAMPLES * SEATS + 2 * SEATS
        assert self.share <= SEATS and self.orders * self.held <= ROWS

    def tables(self):
        fit = regression()
        weight = np.zeros((self.temp_n, self.rows, self.depth), np.float32)
        place = np.full((self.temp_n, self.rows, self.depth), -1.0, np.float32)
        tile_columns = THERMAL_SAMPLES * SEATS
        for device in range(self.temp_n):
            for slot in range(self.cap):
                for order in range(self.orders):
                    row = slot * self.orders + order
                    for t in range(THERMAL_SAMPLES):
                        cells = slice(t * SEATS, (t + 1) * SEATS)
                        weight[device, row, cells] = fit[device * self.orders + order, t]
                        place[device, row, cells] = slot
                row = self.data_rows + slot // 2
                start = tile_columns + (slot % 2) * SEATS
                weight[device, row, start : start + SEATS] = 1.0
                place[device, row, start : start + SEATS] = slot
        both = np.stack([weight, place])
        return both.reshape(2, self.temp_n * self.rows, self.depth)


def line_terms(strength, energy, broad, power, doppler, kelvin):
    inverse = 1.0 / kelvin
    scaled = strength * jnp.exp(energy * (1.0 / REFERENCE_KELVIN - inverse))
    lw = 2.0 * broad * jnp.exp(power * math.log(REFERENCE_KELVIN * inverse))
    gw = (2.35482 * math.sqrt(kelvin / REFERENCE_KELVIN)) * doppler
    g2, l2 = gw * gw, lw * lw
    g3, l3 = g2 * gw, l2 * lw
    g4, l4 = g2 * g2, l2 * l2
    total = (
        g4 * gw
        + 2.69269 * g4 * lw
        + 2.42843 * g3 * l2
        + 4.47163 * g2 * l3
        + 0.07842 * gw * l4
        + l4 * lw
    )
    full = jnp.exp(0.2 * jnp.log(total))
    narrow = 1.0 / full
    share = lw * narrow
    mixing = share * (1.36603 + share * (-0.47719 + share * 0.11116))
    half = 0.5 * full
    lorentz = scaled * mixing * half * (1.0 / math.pi)
    gauss = scaled * (1.0 - mixing) * (0.939437 * narrow)
    slope = (-2.7725887 * math.log2(math.e)) * narrow * narrow
    return half * half, lorentz, slope, gauss


def tile_kernel(
    plan,
    position,
    strength,
    energy,
    broad,
    power,
    doppler,
    window,
    offset,
    owner_slot,
    table,
    sent,
    terms,
    squares,
    mixed,
    tiles,
):
    blocks, temp_n = plan.blocks, plan.temp_n
    me = lax.axis_index("temp").astype(jnp.float32)
    f32 = jnp.float32

    def iota(shape, axis):
        return lax.broadcasted_iota(jnp.int32, shape, axis).astype(f32)

    down, across = iota((blocks, blocks), 0), iota((blocks, blocks), 1)
    eye = down == across

    def stand(row):
        return jnp.sum(jnp.where(eye, row, 0.0), axis=1, keepdims=True)

    def lay(column):
        return jnp.sum(jnp.where(eye, column, 0.0), axis=0, keepdims=True)

    window_column = stand(window[...].astype(f32))
    offset_column = stand(offset[...].astype(f32))
    seat = owner_slot[...].astype(f32)
    slot_column = jnp.sum(
        jnp.where(window_column == iota((blocks, plan.spans), 1), seat, 0.0), axis=1, keepdims=True
    )
    owner_column = jnp.floor((slot_column + 0.5) * (1.0 / plan.held))
    owner_row = lay(owner_column)
    begin_column = (slot_column - owner_column * plan.held) * SPAN_SAMPLES + offset_column
    key_column = owner_column * blocks + iota((blocks, 1), 0)
    key_row = owner_row * blocks + iota((1, blocks), 1)
    rank_row = jnp.sum(jnp.where(key_column < key_row, 1.0, 0.0), axis=0, keepdims=True)
    rank_column = jnp.sum(jnp.where(key_row < key_column, 1.0, 0.0), axis=1, keepdims=True)

    picks = PACK * ROWS
    pick_row = lax.broadcasted_iota(jnp.int32, (picks, blocks), 0)
    quad, piece = pick_row % ROWS, pick_row // ROWS
    local = quad * PACK + piece
    wanted = (local * temp_n).astype(f32) + me
    fits = (quad < plan.quads) & (local < plan.share)
    pick = jnp.where(fits & (rank_row == wanted), 1.0, 0.0)

    def gather(values):
        return jnp.dot(pick, values, precision=HIGHEST, preferred_element_type=f32)

    lane = lax.broadcasted_iota(jnp.int32, (ROWS, LANES), 1)
    segment = lane // PIECE

    def pack(values):
        parts = [values[i * ROWS : (i + 1) * ROWS] for i in range(PACK)]
        out = []
        for j in range(PACK):
            chosen = parts[0]
            for i in range(1, PACK):
                chosen = jnp.where(segment == (i + j) % PACK, parts[i], chosen)
            out.append(chosen if j == 0 else pltpu.roll(chosen, LANES - j * PIECE, 1))
        return out

    begin = gather(jnp.broadcast_to(begin_column, (blocks, LANES)))
    begin_packed = pack(begin)[0]
    columns = [pack(gather(r[...])) for r in (position, strength, energy, broad, power, doppler)]
    for j in range(PACK):
        for t, kelvin in enumerate(kelvins()):
            for k, value in enumerate(line_terms(*(c[j] for c in columns[1:]), kelvin)):
                terms[t, k * PACK + j] = value

    shift = begin_packed - jnp.floor(begin_packed * (1.0 / LANES)) * LANES
    grid = iota((PATCH_SAMPLES, LANES), 0)
    for q in range(plan.quads):
        point = grid - shift[q : q + 1]
        point = jnp.where(point < 0.0, point + PATCH_SAMPLES, point) + 0.5
        for j in range(PACK):
            distance = point - columns[0][j][q : q + 1]
            squares[j] = distance * distance

        def one(t, carry, q=q):
            row = [terms[t, k, pl.ds(q, 1), :] for k in range(4 * PACK)]
            row = [jnp.broadcast_to(r, (ROWS, LANES)) for r in row]
            half2, lorentz = row[:PACK], row[PACK : 2 * PACK]
            slope, gauss = row[2 * PACK : 3 * PACK], row[3 * PACK :]
            for m in range(0, PATCH_SAMPLES, ROWS):
                square = [squares[j, m : m + ROWS, :] for j in range(PACK)]
                below = [square[j] + half2[j] for j in range(PACK)]
                above = list(lorentz)
                while len(below) > 1:
                    above = [
                        above[i] * below[i + 1] + above[i + 1] * below[i]
                        for i in range(0, len(below), 2)
                    ]
                    below = [below[i] * below[i + 1] for i in range(0, len(below), 2)]
                value = above[0] / below[0]
                for j in range(PACK):
                    value = value + gauss[j] * jnp.exp2(slope[j] * square[j])
                mixed[m : m + ROWS, :] = value
            for half in range(0, PATCH_SAMPLES, LANES):
                turned = jnp.transpose(mixed[half : half + LANES, :])
                summed = jnp.sum(turned.reshape(PACK, PIECE, LANES), axis=1)
                tiles[t, q * PACK : (q + 1) * PACK, half : half + LANES] = summed
            return carry

        lax.fori_loop(0, THERMAL_SAMPLES, one, 0)

    depth = plan.depth
    column = lax.broadcasted_iota(jnp.int32, (blocks, depth), 1) % SEATS
    mine = rank_column == (column * temp_n).astype(f32) + me
    real = column < plan.share
    owner_wide = jnp.sum(jnp.where(mine & real, owner_column, 0.0), axis=0, keepdims=True)
    first_wide = jnp.sum(
        jnp.where(owner_column < owner_wide, 1.0, 0.0), axis=0, keepdims=True
    )
    column_row = lax.broadcasted_iota(jnp.int32, (1, depth), 1) % SEATS
    skipped = jnp.floor((first_wide - me + (temp_n - 0.5)) * (1.0 / temp_n))
    place_wide = owner_wide * plan.cap + column_row.astype(f32) - skipped
    place_wide = jnp.where(column_row < plan.share, place_wide, -2.0)

    begins = jnp.concatenate(
        [begin[(n % PACK) * ROWS + n // PACK :][:1] for n in range(plan.quads * PACK)]
        + [jnp.zeros((SEATS - plan.quads * PACK, LANES), f32)]
    )
    if plan.share < SEATS:
        tiles[:, plan.share :, :] = jnp.zeros(
            (THERMAL_SAMPLES, SEATS - plan.share, PATCH_SAMPLES), f32
        )
    nothing = jnp.zeros_like(begins)
    body = jnp.concatenate(
        [
            tiles[...].reshape(THERMAL_SAMPLES * SEATS, PATCH_SAMPLES),
            jnp.concatenate([begins, nothing], axis=1),
            jnp.concatenate([nothing, begins], axis=1),
        ]
    )
    group = temp_n * plan.rows
    weight, place = table[0], table[1]
    for owner in range(plan.lines_n):
        spread = jnp.where(
            (place >= 0.0) & (place + owner * plan.cap == place_wide), weight, 0.0
        )
        sent[owner * group : (owner + 1) * group, :] = jnp.dot(
            spread, body, precision=HIGHEST, preferred_element_type=f32
        )


def place_kernel(plan, got, out):
    f32 = jnp.float32
    senders = plan.lines_n * plan.temp_n
    chunks = SPAN_SAMPLES // LANES
    shape = (senders, plan.rows, LANES)
    both = got[...].reshape(senders, plan.rows, PATCH_SAMPLES)
    left, right = both[:, :, :LANES], both[:, :, LANES:]
    sub = lax.broadcasted_iota(jnp.int32, shape, 1)
    begin = jnp.zeros(shape, f32)
    for slot in range(plan.cap):
        row = plan.data_rows + slot // 2
        source = (right if slot % 2 else left)[:, row : row + 1, :]
        begin = jnp.where(sub // plan.orders == slot, source, begin)
    chunk = jnp.floor(begin * (1.0 / LANES))
    shift = begin - chunk * LANES
    own = jnp.floor(chunk * (1.0 / chunks))
    order = (sub % plan.orders).astype(f32)
    target = (chunk - own * chunks) * ROWS + order * plan.held + own
    lane = lax.broadcasted_iota(jnp.int32, shape, 2).astype(f32)
    hit = jnp.where((sub < plan.data_rows) & (target == lane), 1.0, 0.0)
    early = lane >= shift
    rows = senders * plan.rows
    spread = jnp.concatenate(
        [
            jnp.where(early, left, 0.0).reshape(rows, LANES),
            right.reshape(rows, LANES),
            jnp.where(early, 0.0, left).reshape(rows, LANES),
        ],
        axis=1,
    )
    landed = lax.dot_general(
        hit.reshape(rows, LANES),
        spread,
        (((0,), (0,)), ((), ())),
        precision=HIGHEST,
        preferred_element_type=f32,
    )
    for c in range(chunks):
        total = landed[c * ROWS : (c + 1) * ROWS, :LANES]
        for back in (1, 2):
            if c >= back:
                total = total + landed[
                    (c - back) * ROWS : (c - back + 1) * ROWS, back * LANES : (back + 1) * LANES
                ]
        for order_at in range(plan.orders):
            out[order_at, :, c * LANES : (c + 1) * LANES] = total[
                order_at * plan.held : (order_at + 1) * plan.held
            ]


def on_device(
    line_position,
    line_strength,
    lower_energy,
    broad_width,
    broad_exponent,
    doppler_width,
    block_window,
    tile_offset,
    owner_slot,
):
    plan = Plan(
        lax.axis_size("lines"),
        lax.axis_size("temp"),
        line_position.shape[0],
        owner_slot.shape[0],
    )
    devices = plan.lines_n * plan.temp_n
    f32 = jnp.float32
    sent = pl.pallas_call(
        functools.partial(tile_kernel, plan),
        out_shape=jax.ShapeDtypeStruct((devices * plan.rows, PATCH_SAMPLES), f32),
        scratch_shapes=[
            pltpu.VMEM((THERMAL_SAMPLES, 4 * PACK, ROWS, LANES), f32),
            pltpu.VMEM((PACK, PATCH_SAMPLES, LANES), f32),
            pltpu.VMEM((PATCH_SAMPLES, LANES), f32),
            pltpu.VMEM((THERMAL_SAMPLES, SEATS, PATCH_SAMPLES), f32),
        ],
        name="tiles",
    )(
        line_position,
        line_strength,
        lower_energy,
        broad_width,
        broad_exponent,
        doppler_width,
        block_window[None, :],
        tile_offset[None, :],
        owner_slot[None, :],
        jnp.asarray(plan.tables()),
    )
    got = lax.all_to_all(
        sent.reshape(devices, plan.rows, PATCH_SAMPLES), ("lines", "temp"), 0, 0, tiled=True
    )
    return pl.pallas_call(
        functools.partial(place_kernel, plan),
        out_shape=jax.ShapeDtypeStruct((plan.orders, plan.held, SPAN_SAMPLES), f32),
        name="place",
    )(got.reshape(devices * plan.rows, PATCH_SAMPLES))


def solution(mesh):
    return jax.shard_map(
        on_device,
        mesh=mesh,
        in_specs=(
            P("lines", None),
            P("lines", None),
            P("lines", None),
            P("lines", None),
            P("lines", None),
            P("lines", None),
            P("lines"),
            P("lines"),
            P(),
        ),
        out_specs=P("temp", "lines", None),
        check_vma=False,
    )
```

```python
import functools
import math

import jax
import jax.numpy as jnp
import numpy as np
from jax import lax
from jax.experimental import pallas as pl
from jax.experimental.pallas import tpu as pltpu
from jax.sharding import PartitionSpec as P

LANES = 128
ROWS = 8
PATCH_SAMPLES = 256
SPAN_SAMPLES = 2048
THERMAL_SAMPLES = 8
REFERENCE_KELVIN = 1000.0
PACK = 4
PIECE = LANES // PACK
SEATS = 16
STEP = 16
HIGHEST = lax.Precision.HIGHEST


def kelvins():
    theta = math.pi * (np.arange(THERMAL_SAMPLES) + 0.5) / THERMAL_SAMPLES
    return [float(k) for k in 1650.0 + 1350.0 * np.cos(theta)]


def regression():
    order = np.arange(THERMAL_SAMPLES)
    theta = math.pi * (np.arange(THERMAL_SAMPLES) + 0.5) / THERMAL_SAMPLES
    factor = np.where(order == 0, 1.0, 2.0) / THERMAL_SAMPLES
    return factor[:, None] * np.cos(order[:, None] * theta[None, :])


class Plan:
    def __init__(self, lines_n, temp_n, blocks, spans):
        self.lines_n, self.temp_n, self.blocks, self.spans = lines_n, temp_n, blocks, spans
        self.held = spans // lines_n
        self.orders = THERMAL_SAMPLES // temp_n
        self.share = -(-blocks // temp_n)
        self.quads = -(-self.share // PACK)
        heavy = 3 * ((2 * blocks) // (3 * lines_n))
        self.cap = -(-heavy // temp_n)
        self.lots = self.cap * self.orders
        self.rows = 2 * self.lots + 1
        assert self.share <= SEATS and self.cap <= PACK
        assert self.orders * self.held <= ROWS and ROWS % temp_n == 0

    def table(self):
        weight = regression().astype(np.float32)
        rows = [
            [weight[(d % self.temp_n) * self.orders + order] for d in range(ROWS)]
            for order in range(self.orders)
        ]
        return np.repeat(np.array(rows), SEATS, axis=2)


def line_terms(strength, energy, broad, power, doppler, kelvin):
    inverse = 1.0 / kelvin
    scaled = strength * jnp.exp(energy * (1.0 / REFERENCE_KELVIN - inverse))
    lw = 2.0 * broad * jnp.exp(power * math.log(REFERENCE_KELVIN * inverse))
    gw = (2.35482 * math.sqrt(kelvin / REFERENCE_KELVIN)) * doppler
    g2, l2 = gw * gw, lw * lw
    g3, l3 = g2 * gw, l2 * lw
    g4, l4 = g2 * g2, l2 * l2
    total = (
        g4 * gw
        + 2.69269 * g4 * lw
        + 2.42843 * g3 * l2
        + 4.47163 * g2 * l3
        + 0.07842 * gw * l4
        + l4 * lw
    )
    full = jnp.exp(0.2 * jnp.log(total))
    narrow = 1.0 / full
    share = lw * narrow
    mixing = share * (1.36603 + share * (-0.47719 + share * 0.11116))
    half = 0.5 * full
    lorentz = scaled * mixing * half * (1.0 / math.pi)
    gauss = scaled * (1.0 - mixing) * (0.939437 * narrow)
    slope = (-2.7725887 * math.log2(math.e)) * narrow * narrow
    return half * half, lorentz, slope, gauss


def tile_kernel(
    plan,
    position,
    strength,
    energy,
    broad,
    power,
    doppler,
    window,
    offset,
    owner_slot,
    table,
    sent,
    terms,
    squares,
    mixed,
    tiles,
):
    blocks, temp_n = plan.blocks, plan.temp_n
    me = lax.axis_index("temp").astype(jnp.float32)
    f32 = jnp.float32

    def iota(shape, axis):
        return lax.broadcasted_iota(jnp.int32, shape, axis).astype(f32)

    down, across = iota((blocks, blocks), 0), iota((blocks, blocks), 1)
    eye = down == across

    def stand(row):
        return jnp.sum(jnp.where(eye, row, 0.0), axis=1, keepdims=True)

    def lay(column):
        return jnp.sum(jnp.where(eye, column, 0.0), axis=0, keepdims=True)

    window_column = stand(window[...].astype(f32))
    offset_column = stand(offset[...].astype(f32))
    seat = owner_slot[...].astype(f32)
    slot_column = jnp.sum(
        jnp.where(window_column == iota((blocks, plan.spans), 1), seat, 0.0), axis=1, keepdims=True
    )
    owner_column = jnp.floor((slot_column + 0.5) * (1.0 / plan.held))
    owner_row = lay(owner_column)
    begin_column = (slot_column - owner_column * plan.held) * SPAN_SAMPLES + offset_column
    key_column = owner_column * blocks + iota((blocks, 1), 0)
    key_row = owner_row * blocks + iota((1, blocks), 1)
    rank_row = jnp.sum(jnp.where(key_column < key_row, 1.0, 0.0), axis=0, keepdims=True)
    rank_column = jnp.sum(jnp.where(key_row < key_column, 1.0, 0.0), axis=1, keepdims=True)

    picks = PACK * ROWS
    pick_row = lax.broadcasted_iota(jnp.int32, (picks, blocks), 0)
    quad, piece = pick_row % ROWS, pick_row // ROWS
    local = quad * PACK + piece
    fits = (quad < plan.quads) & (local < plan.share)
    wanted = jnp.where(fits, (local * temp_n).astype(f32) + me, 0.0)
    pick = jnp.where(rank_row == wanted, 1.0, 0.0)

    def gather(values):
        return jnp.dot(pick, values, precision=HIGHEST, preferred_element_type=f32)

    lane = lax.broadcasted_iota(jnp.int32, (ROWS, LANES), 1)
    segment = lane // PIECE

    def pack(values):
        parts = [values[i * ROWS : (i + 1) * ROWS] for i in range(PACK)]
        out = []
        for j in range(PACK):
            chosen = parts[0]
            for i in range(1, PACK):
                chosen = jnp.where(segment == (i + j) % PACK, parts[i], chosen)
            out.append(chosen if j == 0 else pltpu.roll(chosen, LANES - j * PIECE, 1))
        return out

    begin = gather(jnp.broadcast_to(begin_column, (blocks, LANES)))
    begin_packed = pack(begin)[0]
    columns = [pack(gather(r[...])) for r in (position, strength, energy, broad, power, doppler)]
    for j in range(PACK):
        for t, kelvin in enumerate(kelvins()):
            for k, value in enumerate(line_terms(*(c[j] for c in columns[1:]), kelvin)):
                terms[t, k * PACK + j] = value

    shift = begin_packed - jnp.floor(begin_packed * (1.0 / LANES)) * LANES
    grid = iota((PATCH_SAMPLES, LANES), 0)
    for q in range(plan.quads):
        point = grid - shift[q : q + 1]
        point = jnp.where(point < 0.0, point + PATCH_SAMPLES, point) + 0.5
        for j in range(PACK):
            distance = point - columns[0][j][q : q + 1]
            squares[q * PACK + j] = distance * distance

    width = 2 * plan.quads * LANES
    across_lines = lax.broadcasted_iota(jnp.int32, (SEATS, width), 1)
    seat_of = across_lines // (2 * LANES) * PACK + across_lines % LANES // PIECE
    seats = jnp.where(
        (seat_of == lax.broadcasted_iota(jnp.int32, (SEATS, width), 0)) & (seat_of < plan.share),
        1.0,
        0.0,
    ).astype(jnp.bfloat16)

    def one(t, carry):
        for q in range(plan.quads):
            row = [terms[t, k, pl.ds(q, 1), :] for k in range(4 * PACK)]
            row = [jnp.broadcast_to(r, (STEP, LANES)) for r in row]
            half2, lorentz = row[:PACK], row[PACK : 2 * PACK]
            slope, gauss = row[2 * PACK : 3 * PACK], row[3 * PACK :]
            for m in range(0, PATCH_SAMPLES, STEP):
                square = [squares[q * PACK + j, m : m + STEP, :] for j in range(PACK)]
                below = [square[j] + half2[j] for j in range(PACK)]
                above = list(lorentz)
                while len(below) > 1:
                    above = [
                        above[i] * below[i + 1] + above[i + 1] * below[i]
                        for i in range(0, len(below), 2)
                    ]
                    below = [below[i] * below[i + 1] for i in range(0, len(below), 2)]
                value = above[0] / below[0]
                for j in range(PACK):
                    value = value + gauss[j] * jnp.exp2(slope[j] * square[j])
                high = value.astype(jnp.bfloat16)
                low = (value - high.astype(f32)).astype(jnp.bfloat16)
                mixed[m : m + STEP, 2 * q * LANES : (2 * q + 1) * LANES] = high
                mixed[m : m + STEP, (2 * q + 1) * LANES : (2 * q + 2) * LANES] = low
        tiles[t] = lax.dot_general(
            seats,
            mixed[...],
            (((1,), (1,)), ((), ())),
            preferred_element_type=f32,
        )
        return carry

    lax.fori_loop(0, THERMAL_SAMPLES, one, 0, unroll=4)

    depth = THERMAL_SAMPLES * SEATS
    column = lax.broadcasted_iota(jnp.int32, (blocks, depth), 1) % SEATS
    mine = rank_column == (column * temp_n).astype(f32) + me
    real = column < plan.share
    owner_wide = jnp.sum(jnp.where(mine & real, owner_column, 0.0), axis=0, keepdims=True)
    first_wide = jnp.sum(
        jnp.where(owner_column < owner_wide, 1.0, 0.0), axis=0, keepdims=True
    )
    column_row = lax.broadcasted_iota(jnp.int32, (1, depth), 1) % SEATS
    skipped = jnp.floor((first_wide - me + (temp_n - 0.5)) * (1.0 / temp_n))
    place_wide = owner_wide * plan.cap + column_row.astype(f32) - skipped
    place_wide = jnp.where(column_row < plan.share, place_wide, -2.0)

    begins = jnp.concatenate(
        [begin[(n % PACK) * ROWS + n // PACK :][:1] for n in range(plan.quads * PACK)]
        + [jnp.zeros((SEATS - plan.quads * PACK, LANES), f32)] * (SEATS > plan.quads * PACK)
    )
    devices = plan.lines_n * temp_n
    receiver = lax.broadcasted_iota(jnp.int32, (devices, depth), 0)
    owner_place = (receiver // temp_n * plan.cap).astype(f32)
    placed = [owner_place + slot == place_wide for slot in range(plan.cap)]
    spread = []
    for slot in range(plan.cap):
        for order in range(plan.orders):
            weight = jnp.concatenate([table[order]] * (devices // ROWS))
            spread.append(jnp.where(placed[slot], weight, 0.0))
    coefficients = jnp.dot(
        jnp.concatenate(spread),
        tiles[...].reshape(depth, PATCH_SAMPLES),
        precision=HIGHEST,
        preferred_element_type=f32,
    )
    for lot in range(plan.lots):
        for half in range(2):
            sent[pl.ds(2 * lot + half, devices, stride=plan.rows), :] = coefficients[
                lot * devices : (lot + 1) * devices, half * LANES : (half + 1) * LANES
            ]
    held_lane = lax.broadcasted_iota(jnp.int32, (SEATS, LANES), 1) // PIECE
    where_to = jnp.zeros((devices, LANES), f32)
    for slot in range(plan.cap):
        where_to = where_to + jnp.dot(
            jnp.where(placed[slot][:, :SEATS], 1.0, 0.0),
            jnp.where(held_lane == slot, begins, 0.0),
            precision=HIGHEST,
            preferred_element_type=f32,
        )
    sent[pl.ds(2 * plan.lots, devices, stride=plan.rows), :] = where_to


def place_kernel(plan, got, out):
    f32 = jnp.float32
    senders = plan.lines_n * plan.temp_n
    chunks = SPAN_SAMPLES // LANES
    lane = lax.broadcasted_iota(jnp.int32, (senders, LANES), 1).astype(f32)

    def take(row):
        return got[pl.ds(row, senders, stride=plan.rows), :]

    begins = take(2 * plan.lots)
    hits, spread = [], []
    for slot in range(plan.cap):
        begin = begins[:, slot * PIECE : slot * PIECE + 1]
        chunk = jnp.floor(begin * (1.0 / LANES))
        own = jnp.floor(chunk * (1.0 / chunks))
        early = lane >= begin - chunk * LANES
        target = (chunk - own * chunks) * ROWS + own
        for order in range(plan.orders):
            lot = slot * plan.orders + order
            left, right = take(2 * lot), take(2 * lot + 1)
            hits.append(jnp.where(target + order * plan.held == lane, 1.0, 0.0))
            spread.append(
                jnp.concatenate(
                    [jnp.where(early, left, 0.0), right, jnp.where(early, 0.0, left)], axis=1
                )
            )
    landed = lax.dot_general(
        jnp.concatenate(hits),
        jnp.concatenate(spread),
        (((0,), (0,)), ((), ())),
        precision=HIGHEST,
        preferred_element_type=f32,
    )
    for c in range(chunks):
        total = landed[c * ROWS : (c + 1) * ROWS, :LANES]
        for back in (1, 2):
            if c >= back:
                total = total + landed[
                    (c - back) * ROWS : (c - back + 1) * ROWS, back * LANES : (back + 1) * LANES
                ]
        for order_at in range(plan.orders):
            out[order_at, :, c * LANES : (c + 1) * LANES] = total[
                order_at * plan.held : (order_at + 1) * plan.held
            ]


def on_device(
    line_position,
    line_strength,
    lower_energy,
    broad_width,
    broad_exponent,
    doppler_width,
    block_window,
    tile_offset,
    owner_slot,
):
    plan = Plan(
        lax.axis_size("lines"),
        lax.axis_size("temp"),
        line_position.shape[0],
        owner_slot.shape[0],
    )
    devices = plan.lines_n * plan.temp_n
    f32 = jnp.float32
    sent = pl.pallas_call(
        functools.partial(tile_kernel, plan),
        out_shape=pltpu.VMEM((devices * plan.rows, LANES), f32),
        scratch_shapes=[
            pltpu.VMEM((THERMAL_SAMPLES, 4 * PACK, ROWS, LANES), f32),
            pltpu.VMEM((plan.quads * PACK, PATCH_SAMPLES, LANES), f32),
            pltpu.VMEM((PATCH_SAMPLES, 2 * plan.quads * LANES), jnp.bfloat16),
            pltpu.VMEM((THERMAL_SAMPLES, SEATS, PATCH_SAMPLES), f32),
        ],
        name="tiles",
    )(
        line_position,
        line_strength,
        lower_energy,
        broad_width,
        broad_exponent,
        doppler_width,
        block_window[None, :],
        tile_offset[None, :],
        owner_slot[None, :],
        jnp.asarray(plan.table()),
    )
    got = lax.all_to_all(
        sent.reshape(devices, 1, plan.rows * LANES), ("lines", "temp"), 0, 0, tiled=True
    )
    return pl.pallas_call(
        functools.partial(place_kernel, plan),
        out_shape=jax.ShapeDtypeStruct((plan.orders, plan.held, SPAN_SAMPLES), f32),
        name="place",
    )(pltpu.with_memory_space_constraint(got.reshape(devices * plan.rows, LANES), pltpu.VMEM))


def solution(mesh):
    return jax.shard_map(
        on_device,
        mesh=mesh,
        in_specs=(
            P("lines", None),
            P("lines", None),
            P("lines", None),
            P("lines", None),
            P("lines", None),
            P("lines", None),
            P("lines"),
            P("lines"),
            P(),
        ),
        out_specs=P("temp", "lines", None),
        check_vma=False,
    )
```

```python
import functools
import math

import jax
import jax.numpy as jnp
import numpy as np
from jax import lax
from jax.experimental import pallas as pl
from jax.experimental.pallas import tpu as pltpu
from jax.sharding import PartitionSpec as P

LANES = 128
ROWS = 8
PATCH_SAMPLES = 256
SPAN_SAMPLES = 2048
THERMAL_SAMPLES = 8
REFERENCE_KELVIN = 1000.0
PIECE = 32
SEATS = 16
GROUP = 8
STEP = 16
HIGHEST = lax.Precision.HIGHEST


def kelvins():
    theta = math.pi * (np.arange(THERMAL_SAMPLES) + 0.5) / THERMAL_SAMPLES
    return [float(k) for k in 1650.0 + 1350.0 * np.cos(theta)]


def regression():
    order = np.arange(THERMAL_SAMPLES)
    theta = math.pi * (np.arange(THERMAL_SAMPLES) + 0.5) / THERMAL_SAMPLES
    factor = np.where(order == 0, 1.0, 2.0) / THERMAL_SAMPLES
    return factor[:, None] * np.cos(order[:, None] * theta[None, :])


class Plan:
    def __init__(self, lines_n, temp_n, blocks, spans):
        self.lines_n, self.temp_n, self.blocks, self.spans = lines_n, temp_n, blocks, spans
        self.held = spans // lines_n
        self.orders = THERMAL_SAMPLES // temp_n
        self.share = -(-blocks // temp_n)
        self.groups, first = [], 0
        while first < self.share:
            size = min(GROUP, 2 ** int(math.log2(self.share - first)))
            self.groups.append((first, size))
            first += size
        heavy = 3 * ((2 * blocks) // (3 * lines_n))
        self.cap = -(-heavy // temp_n)
        self.lots = self.cap * self.orders
        self.rows = 2 * self.lots + 1
        assert self.share <= SEATS and self.cap <= LANES // PIECE and blocks % temp_n == 0
        assert self.orders * self.held <= ROWS and ROWS % temp_n == 0

    def table(self):
        weight = regression().astype(np.float32)
        rows = [
            [weight[(d % self.temp_n) * self.orders + order] for d in range(ROWS)]
            for order in range(self.orders)
        ]
        return np.repeat(np.array(rows), SEATS, axis=2)


def line_terms(strength, energy, broad, power, doppler, kelvin):
    inverse = 1.0 / kelvin
    scaled = strength * jnp.exp(energy * (1.0 / REFERENCE_KELVIN - inverse))
    lw = 2.0 * broad * jnp.exp(power * math.log(REFERENCE_KELVIN * inverse))
    gw = (2.35482 * math.sqrt(kelvin / REFERENCE_KELVIN)) * doppler
    g2, l2 = gw * gw, lw * lw
    g3, l3 = g2 * gw, l2 * lw
    g4, l4 = g2 * g2, l2 * l2
    total = (
        g4 * gw
        + 2.69269 * g4 * lw
        + 2.42843 * g3 * l2
        + 4.47163 * g2 * l3
        + 0.07842 * gw * l4
        + l4 * lw
    )
    full = jnp.exp(0.2 * jnp.log(total))
    narrow = 1.0 / full
    share = lw * narrow
    mixing = share * (1.36603 + share * (-0.47719 + share * 0.11116))
    lorentz = (-2.0 / math.pi) * narrow * scaled * mixing
    gauss = (2.0 * 0.939437) * narrow * scaled * (1.0 - mixing)
    return -4.0 * narrow * narrow, lorentz, gauss


def split(values, parts):
    out = []
    for part in range(parts):
        out.append(values.astype(jnp.bfloat16))
        if part < parts - 1:
            values = values - out[-1].astype(jnp.float32)
    return out


def choose(ones, values, parts):
    return jnp.dot(
        jnp.concatenate([ones.astype(jnp.bfloat16)] * parts, axis=1),
        jnp.concatenate(split(values, parts)),
        preferred_element_type=jnp.float32,
    )


def tile_kernel(
    plan,
    position,
    strength,
    energy,
    broad,
    power,
    doppler,
    window,
    offset,
    owner_slot,
    table,
    sent,
    terms,
    squares,
    mixed,
    tiles,
    spread,
):
    blocks, temp_n = plan.blocks, plan.temp_n
    me = lax.axis_index("temp").astype(jnp.float32)
    f32 = jnp.float32

    def iota(shape, axis):
        return lax.broadcasted_iota(jnp.int32, shape, axis).astype(f32)

    down, across = iota((blocks, blocks), 0), iota((blocks, blocks), 1)
    eye = down == across

    def stand(row):
        return jnp.sum(jnp.where(eye, row, 0.0), axis=1, keepdims=True)

    def lay(column):
        return jnp.sum(jnp.where(eye, column, 0.0), axis=0, keepdims=True)

    window_column = stand(window[...].astype(f32))
    offset_column = stand(offset[...].astype(f32))
    seat = owner_slot[...].astype(f32)
    slot_column = jnp.sum(
        jnp.where(window_column == iota((blocks, plan.spans), 1), seat, 0.0), axis=1, keepdims=True
    )
    owner_column = jnp.floor((slot_column + 0.5) * (1.0 / plan.held))
    owner_row = lay(owner_column)
    begin_column = (slot_column - owner_column * plan.held) * SPAN_SAMPLES + offset_column
    key_column = owner_column * blocks + iota((blocks, 1), 0)
    key_row = owner_row * blocks + iota((1, blocks), 1)
    rank_row = jnp.sum(jnp.where(key_column < key_row, 1.0, 0.0), axis=0, keepdims=True)
    rank_column = jnp.sum(jnp.where(key_row < key_column, 1.0, 0.0), axis=1, keepdims=True)

    picks = len(plan.groups) * ROWS
    pick_row = lax.broadcasted_iota(jnp.int32, (picks, blocks), 0)
    local = jnp.zeros((picks, blocks), jnp.int32)
    for g, (first, size) in enumerate(plan.groups):
        local = jnp.where(pick_row // ROWS == g, first + pick_row % size, local)
    pick = jnp.where(rank_row == (local * temp_n).astype(f32) + me, 1.0, 0.0)

    def gather(values):
        return choose(pick, values, 3)

    row = lax.broadcasted_iota(jnp.int32, (ROWS, LANES), 0)
    lane = lax.broadcasted_iota(jnp.int32, (ROWS, LANES), 1)

    def pack(values):
        out = []
        for g, (_, size) in enumerate(plan.groups):
            part = values[g * ROWS : (g + 1) * ROWS]
            width = LANES // size
            for bit in range(size.bit_length() - 1):
                step = 1 << bit
                turned = pltpu.roll(part, ROWS - step, 0)
                part = jnp.where(lane // width & step != 0, turned, part)
            for bit in range(size.bit_length() - 1):
                step = 1 << bit
                turned = pltpu.roll(part, step * width, 1)
                part = jnp.where(row & step != 0, turned, part)
            out.append(part)
        return out

    begin = gather(jnp.broadcast_to(begin_column, (blocks, LANES)))
    columns = [pack(gather(r[...])) for r in (position, strength, energy, broad, power, doppler)]
    begin_packed = pack(begin)
    for g in range(len(plan.groups)):
        for t, kelvin in enumerate(kelvins()):
            for k, value in enumerate(line_terms(*(c[g] for c in columns[1:]), kelvin)):
                terms[t, k, g * ROWS : (g + 1) * ROWS] = value

    depth = THERMAL_SAMPLES * SEATS
    column = lax.broadcasted_iota(jnp.int32, (blocks, depth), 1) % SEATS
    mine = rank_column == (column * temp_n).astype(f32) + me
    real = column < plan.share
    owner_wide = jnp.sum(jnp.where(mine & real, owner_column, 0.0), axis=0, keepdims=True)
    first_wide = jnp.sum(
        jnp.where(owner_column < owner_wide, 1.0, 0.0), axis=0, keepdims=True
    )
    column_row = lax.broadcasted_iota(jnp.int32, (1, depth), 1) % SEATS
    skipped = jnp.floor((first_wide - me + (temp_n - 0.5)) * (1.0 / temp_n))
    place_wide = owner_wide * plan.cap + column_row.astype(f32) - skipped
    place_wide = jnp.where(column_row < plan.share, place_wide, -2.0)

    begins = jnp.concatenate(
        [begin[g * ROWS : g * ROWS + size] for g, (_, size) in enumerate(plan.groups)]
        + [jnp.zeros((SEATS - plan.share, LANES), f32)] * (SEATS > plan.share)
    )
    devices = plan.lines_n * temp_n
    receiver = lax.broadcasted_iota(jnp.int32, (devices, depth), 0)
    owner_place = (receiver // temp_n * plan.cap).astype(f32)
    placed = [owner_place + slot == place_wide for slot in range(plan.cap)]
    for slot in range(plan.cap):
        for order in range(plan.orders):
            weight = jnp.concatenate([table[order]] * (devices // ROWS))
            lot = slot * plan.orders + order
            spread[lot * devices : (lot + 1) * devices, :] = jnp.where(placed[slot], weight, 0.0)
    held_lane = lax.broadcasted_iota(jnp.int32, (SEATS, LANES), 1) // PIECE
    sent[pl.ds(2 * plan.lots, devices, stride=plan.rows), :] = choose(
        jnp.concatenate([jnp.where(p[:, :SEATS], 1.0, 0.0) for p in placed], axis=1),
        jnp.concatenate(
            [jnp.where(held_lane == slot, begins, 0.0) for slot in range(plan.cap)]
        ),
        2,
    )

    grid = iota((PATCH_SAMPLES, LANES), 0)
    for g, (first, size) in enumerate(plan.groups):
        start = begin_packed[g][:1]
        point = grid - (start - jnp.floor(start * (1.0 / LANES)) * LANES)
        point = jnp.where(point < 0.0, point + PATCH_SAMPLES, point) + 0.5
        for j in range(size):
            distance = point - columns[0][g][j : j + 1]
            squares[first + j] = distance * distance

    width = 2 * LANES * len(plan.groups)
    held_by = lax.broadcasted_iota(jnp.int32, (SEATS, width), 1)
    seat_of = jnp.zeros((SEATS, width), jnp.int32)
    for g, (first, size) in enumerate(plan.groups):
        seat = first + held_by % LANES // (LANES // size)
        seat_of = jnp.where(held_by // (2 * LANES) == g, seat, seat_of)
    seats = jnp.where(
        seat_of == lax.broadcasted_iota(jnp.int32, (SEATS, width), 0), 1.0, 0.0
    ).astype(jnp.bfloat16)

    def one(t, carry):
        for g, (first, size) in enumerate(plan.groups):
            rows = [
                [
                    jnp.broadcast_to(terms[t, k, g * ROWS + j : g * ROWS + j + 1, :], (STEP, LANES))
                    for k in range(3)
                ]
                for j in range(size)
            ]
            for m in range(0, PATCH_SAMPLES, STEP):
                value = None
                for j, (scale, lorentz, gauss) in enumerate(rows):
                    reach = squares[first + j, m : m + STEP, :] * scale - 1.0
                    term = lorentz / reach + gauss * jnp.exp2(reach)
                    value = term if value is None else value + term
                high = value.astype(jnp.bfloat16)
                low = (value - high.astype(f32)).astype(jnp.bfloat16)
                mixed[m : m + STEP, 2 * g * LANES : (2 * g + 1) * LANES] = high
                mixed[m : m + STEP, (2 * g + 1) * LANES : (2 * g + 2) * LANES] = low
        for half in range(0, PATCH_SAMPLES, LANES):
            tiles[t, :, half : half + LANES] = lax.dot_general(
                seats,
                mixed[half : half + LANES, :],
                (((1,), (1,)), ((), ())),
                preferred_element_type=f32,
            )
        return carry

    lax.fori_loop(0, THERMAL_SAMPLES, one, 0, unroll=4)

    coefficients = jnp.dot(
        spread[...],
        tiles[...].reshape(depth, PATCH_SAMPLES),
        precision=HIGHEST,
        preferred_element_type=f32,
    )
    for lot in range(plan.lots):
        for half in range(2):
            sent[pl.ds(2 * lot + half, devices, stride=plan.rows), :] = coefficients[
                lot * devices : (lot + 1) * devices, half * LANES : (half + 1) * LANES
            ]


def place_kernel(plan, got, out):
    f32 = jnp.float32
    senders = plan.lines_n * plan.temp_n
    chunks = SPAN_SAMPLES // LANES
    lane = lax.broadcasted_iota(jnp.int32, (senders, LANES), 1).astype(f32)

    def take(row):
        return got[pl.ds(row, senders, stride=plan.rows), :]

    begins = take(2 * plan.lots)
    hits, spread = [], []
    for slot in range(plan.cap):
        begin = begins[:, slot * PIECE : slot * PIECE + 1]
        chunk = jnp.floor(begin * (1.0 / LANES))
        own = jnp.floor(chunk * (1.0 / chunks))
        early = lane >= begin - chunk * LANES
        target = (chunk - own * chunks) * ROWS + own
        for order in range(plan.orders):
            lot = slot * plan.orders + order
            left, right = take(2 * lot), take(2 * lot + 1)
            hits.append(jnp.where(target + order * plan.held == lane, 1.0, 0.0))
            spread.append(
                jnp.concatenate(
                    [jnp.where(early, left, 0.0), right, jnp.where(early, 0.0, left)], axis=1
                )
            )
    landed = lax.dot_general(
        jnp.concatenate([jnp.concatenate(hits).astype(jnp.bfloat16)] * 3),
        jnp.concatenate(split(jnp.concatenate(spread), 3)),
        (((0,), (0,)), ((), ())),
        preferred_element_type=f32,
    )
    for c in range(chunks):
        total = landed[c * ROWS : (c + 1) * ROWS, :LANES]
        for back in (1, 2):
            if c >= back:
                total = total + landed[
                    (c - back) * ROWS : (c - back + 1) * ROWS, back * LANES : (back + 1) * LANES
                ]
        for order_at in range(plan.orders):
            out[order_at, :, c * LANES : (c + 1) * LANES] = total[
                order_at * plan.held : (order_at + 1) * plan.held
            ]


def on_device(
    line_position,
    line_strength,
    lower_energy,
    broad_width,
    broad_exponent,
    doppler_width,
    block_window,
    tile_offset,
    owner_slot,
):
    plan = Plan(
        lax.axis_size("lines"),
        lax.axis_size("temp"),
        line_position.shape[0],
        owner_slot.shape[0],
    )
    devices = plan.lines_n * plan.temp_n
    f32 = jnp.float32
    sent = pl.pallas_call(
        functools.partial(tile_kernel, plan),
        out_shape=pltpu.VMEM((devices * plan.rows, LANES), f32),
        scratch_shapes=[
            pltpu.VMEM((THERMAL_SAMPLES, 3, len(plan.groups) * ROWS, LANES), f32),
            pltpu.VMEM((plan.share, PATCH_SAMPLES, LANES), f32),
            pltpu.VMEM((PATCH_SAMPLES, 2 * LANES * len(plan.groups)), jnp.bfloat16),
            pltpu.VMEM((THERMAL_SAMPLES, SEATS, PATCH_SAMPLES), f32),
            pltpu.VMEM((plan.lots * devices, THERMAL_SAMPLES * SEATS), f32),
        ],
        name="tiles",
    )(
        line_position,
        line_strength,
        lower_energy,
        broad_width,
        broad_exponent,
        doppler_width,
        block_window[None, :],
        tile_offset[None, :],
        owner_slot[None, :],
        jnp.asarray(plan.table()),
    )
    got = lax.all_to_all(
        sent.reshape(devices, 1, plan.rows * LANES), ("lines", "temp"), 0, 0, tiled=True
    )
    return pl.pallas_call(
        functools.partial(place_kernel, plan),
        out_shape=jax.ShapeDtypeStruct((plan.orders, plan.held, SPAN_SAMPLES), f32),
        name="place",
    )(pltpu.with_memory_space_constraint(got.reshape(devices * plan.rows, LANES), pltpu.VMEM))


def solution(mesh):
    return jax.shard_map(
        on_device,
        mesh=mesh,
        in_specs=(
            P("lines", None),
            P("lines", None),
            P("lines", None),
            P("lines", None),
            P("lines", None),
            P("lines", None),
            P("lines"),
            P("lines"),
            P(),
        ),
        out_specs=P("temp", "lines", None),
        check_vma=False,
    )
```

```python
import functools
import math

import jax
import jax.numpy as jnp
import numpy as np
from jax import lax
from jax.experimental import pallas as pl
from jax.experimental.pallas import tpu as pltpu
from jax.sharding import PartitionSpec as P

LANES = 128
ROWS = 8
PATCH_SAMPLES = 256
SPAN_SAMPLES = 2048
THERMAL_SAMPLES = 8
REFERENCE_KELVIN = 1000.0
PIECE = 32
SEATS = 16
GROUP = 8
STEP = 16
HIGHEST = lax.Precision.HIGHEST


def kelvins():
    theta = math.pi * (np.arange(THERMAL_SAMPLES) + 0.5) / THERMAL_SAMPLES
    return [float(k) for k in 1650.0 + 1350.0 * np.cos(theta)]


def regression():
    order = np.arange(THERMAL_SAMPLES)
    theta = math.pi * (np.arange(THERMAL_SAMPLES) + 0.5) / THERMAL_SAMPLES
    factor = np.where(order == 0, 1.0, 2.0) / THERMAL_SAMPLES
    return factor[:, None] * np.cos(order[:, None] * theta[None, :])


class Plan:
    def __init__(self, lines_n, temp_n, blocks, spans):
        self.lines_n, self.temp_n, self.blocks, self.spans = lines_n, temp_n, blocks, spans
        self.held = spans // lines_n
        self.orders = THERMAL_SAMPLES // temp_n
        self.share = -(-blocks // temp_n)
        self.groups, first = [], 0
        while first < self.share:
            size = min(GROUP, 2 ** int(math.log2(self.share - first)))
            self.groups.append((first, size))
            first += size
        heavy = 3 * ((2 * blocks) // (3 * lines_n))
        self.cap = -(-heavy // temp_n)
        self.lots = self.cap * self.orders
        self.rows = 2 * self.lots + 1
        assert self.share <= SEATS and self.cap <= LANES // PIECE and blocks % temp_n == 0
        assert self.orders * self.held <= ROWS and ROWS % temp_n == 0

    def table(self):
        weight = regression().astype(np.float32)
        rows = [
            [weight[(d % self.temp_n) * self.orders + order] for d in range(ROWS)]
            for order in range(self.orders)
        ]
        return np.repeat(np.array(rows), SEATS, axis=2)


def line_terms(strength, energy, broad, power, doppler, kelvin):
    inverse = 1.0 / kelvin
    scaled = strength * jnp.exp(energy * (1.0 / REFERENCE_KELVIN - inverse))
    lw = 2.0 * broad * jnp.exp(power * math.log(REFERENCE_KELVIN * inverse))
    gw = (2.35482 * math.sqrt(kelvin / REFERENCE_KELVIN)) * doppler
    g2, l2 = gw * gw, lw * lw
    g3, l3 = g2 * gw, l2 * lw
    g4, l4 = g2 * g2, l2 * l2
    total = (
        g4 * gw
        + 2.69269 * g4 * lw
        + 2.42843 * g3 * l2
        + 4.47163 * g2 * l3
        + 0.07842 * gw * l4
        + l4 * lw
    )
    full = jnp.exp(0.2 * jnp.log(total))
    narrow = 1.0 / full
    share = lw * narrow
    mixing = share * (1.36603 + share * (-0.47719 + share * 0.11116))
    lorentz = (-2.0 / math.pi) * narrow * scaled * mixing
    gauss = (2.0 * 0.939437) * narrow * scaled * (1.0 - mixing)
    return -4.0 * narrow * narrow, lorentz, gauss


def split(values, parts):
    out = []
    for part in range(parts):
        out.append(values.astype(jnp.bfloat16))
        if part < parts - 1:
            values = values - out[-1].astype(jnp.float32)
    return out


def choose(ones, values, parts):
    return jnp.dot(
        jnp.concatenate([ones.astype(jnp.bfloat16)] * parts, axis=1),
        jnp.concatenate(split(values, parts)),
        preferred_element_type=jnp.float32,
    )


def tile_kernel(
    plan,
    position,
    strength,
    energy,
    broad,
    power,
    doppler,
    window,
    offset,
    owner_slot,
    table,
    sent,
    terms,
    squares,
    mixed,
    tiles,
    spread,
):
    blocks, temp_n = plan.blocks, plan.temp_n
    me = lax.axis_index("temp").astype(jnp.float32)
    f32 = jnp.float32

    def iota(shape, axis):
        return lax.broadcasted_iota(jnp.int32, shape, axis).astype(f32)

    down, across = iota((blocks, blocks), 0), iota((blocks, blocks), 1)
    eye = down == across

    def stand(row):
        return jnp.sum(jnp.where(eye, row, 0.0), axis=1, keepdims=True)

    def lay(column):
        return jnp.sum(jnp.where(eye, column, 0.0), axis=0, keepdims=True)

    window_column = stand(window[...].astype(f32))
    offset_column = stand(offset[...].astype(f32))
    seat = owner_slot[...].astype(f32)
    slot_column = jnp.sum(
        jnp.where(window_column == iota((blocks, plan.spans), 1), seat, 0.0), axis=1, keepdims=True
    )
    owner_column = jnp.floor((slot_column + 0.5) * (1.0 / plan.held))
    owner_row = lay(owner_column)
    begin_column = (slot_column - owner_column * plan.held) * SPAN_SAMPLES + offset_column
    key_column = owner_column * blocks + iota((blocks, 1), 0)
    key_row = owner_row * blocks + iota((1, blocks), 1)
    rank_row = jnp.sum(jnp.where(key_column < key_row, 1.0, 0.0), axis=0, keepdims=True)
    rank_column = jnp.sum(jnp.where(key_row < key_column, 1.0, 0.0), axis=1, keepdims=True)

    picks = len(plan.groups) * ROWS
    pick_row = lax.broadcasted_iota(jnp.int32, (picks, blocks), 0)
    local = jnp.zeros((picks, blocks), jnp.int32)
    for g, (first, size) in enumerate(plan.groups):
        local = jnp.where(pick_row // ROWS == g, first + pick_row % size, local)
    pick = jnp.where(rank_row == (local * temp_n).astype(f32) + me, 1.0, 0.0)

    def gather(values):
        return choose(pick, values, 3)

    row = lax.broadcasted_iota(jnp.int32, (ROWS, LANES), 0)
    lane = lax.broadcasted_iota(jnp.int32, (ROWS, LANES), 1)

    def pack(values):
        out = []
        for g, (_, size) in enumerate(plan.groups):
            part = values[g * ROWS : (g + 1) * ROWS]
            width = LANES // size
            for bit in range(size.bit_length() - 1):
                step = 1 << bit
                turned = pltpu.roll(part, ROWS - step, 0)
                part = jnp.where(lane // width & step != 0, turned, part)
            for bit in range(size.bit_length() - 1):
                step = 1 << bit
                turned = pltpu.roll(part, step * width, 1)
                part = jnp.where(row & step != 0, turned, part)
            out.append(part)
        return out

    begin = gather(jnp.broadcast_to(begin_column, (blocks, LANES)))
    every = [r[...] for r in (position, strength, energy, broad, power, doppler)]
    every = gather(jnp.concatenate(every, axis=1))
    columns = [pack(every[:, i * LANES : (i + 1) * LANES]) for i in range(6)]
    begin_packed = pack(begin)
    for g in range(len(plan.groups)):
        for t, kelvin in enumerate(kelvins()):
            for k, value in enumerate(line_terms(*(c[g] for c in columns[1:]), kelvin)):
                terms[t, k, g * ROWS : (g + 1) * ROWS] = value

    depth = THERMAL_SAMPLES * SEATS
    column = lax.broadcasted_iota(jnp.int32, (blocks, depth), 1) % SEATS
    mine = rank_column == (column * temp_n).astype(f32) + me
    real = column < plan.share
    owner_wide = jnp.sum(jnp.where(mine & real, owner_column, 0.0), axis=0, keepdims=True)
    first_wide = jnp.sum(
        jnp.where(owner_column < owner_wide, 1.0, 0.0), axis=0, keepdims=True
    )
    column_row = lax.broadcasted_iota(jnp.int32, (1, depth), 1) % SEATS
    skipped = jnp.floor((first_wide - me + (temp_n - 0.5)) * (1.0 / temp_n))
    place_wide = owner_wide * plan.cap + column_row.astype(f32) - skipped
    place_wide = jnp.where(column_row < plan.share, place_wide, -2.0)

    begins = jnp.concatenate(
        [begin[g * ROWS : g * ROWS + size] for g, (_, size) in enumerate(plan.groups)]
        + [jnp.zeros((SEATS - plan.share, LANES), f32)] * (SEATS > plan.share)
    )
    devices = plan.lines_n * temp_n
    receiver = lax.broadcasted_iota(jnp.int32, (devices, depth), 0)
    owner_place = (receiver // temp_n * plan.cap).astype(f32)
    placed = [owner_place + slot == place_wide for slot in range(plan.cap)]
    for slot in range(plan.cap):
        for order in range(plan.orders):
            weight = jnp.concatenate([table[order]] * (devices // ROWS))
            lot = slot * plan.orders + order
            high, low = split(jnp.where(placed[slot], weight, 0.0), 2)
            spread[lot * devices : (lot + 1) * devices, :] = jnp.concatenate(
                [high, low, high], axis=1
            )
    held_lane = lax.broadcasted_iota(jnp.int32, (SEATS, LANES), 1) // PIECE
    sent[pl.ds(2 * plan.lots, devices, stride=plan.rows), :] = choose(
        jnp.concatenate([jnp.where(p[:, :SEATS], 1.0, 0.0) for p in placed], axis=1),
        jnp.concatenate(
            [jnp.where(held_lane == slot, begins, 0.0) for slot in range(plan.cap)]
        ),
        2,
    )

    grid = iota((PATCH_SAMPLES, LANES), 0)
    for g, (first, size) in enumerate(plan.groups):
        start = begin_packed[g][:1]
        point = grid - (start - jnp.floor(start * (1.0 / LANES)) * LANES)
        point = jnp.where(point < 0.0, point + PATCH_SAMPLES, point) + 0.5
        for j in range(size):
            distance = point - columns[0][g][j : j + 1]
            squares[first + j] = distance * distance

    width = 2 * LANES * len(plan.groups)
    held_by = lax.broadcasted_iota(jnp.int32, (SEATS, width), 1)
    seat_of = jnp.zeros((SEATS, width), jnp.int32)
    for g, (first, size) in enumerate(plan.groups):
        seat = first + held_by % LANES // (LANES // size)
        seat_of = jnp.where(held_by // (2 * LANES) == g, seat, seat_of)
    seats = jnp.where(
        seat_of == lax.broadcasted_iota(jnp.int32, (SEATS, width), 0), 1.0, 0.0
    ).astype(jnp.bfloat16)

    def one(t, carry):
        part = PATCH_SAMPLES // 2
        for half in range(0, PATCH_SAMPLES, part):
            for g, (first, size) in enumerate(plan.groups):
                rows = [
                    [
                        jnp.broadcast_to(
                            terms[t, k, g * ROWS + j : g * ROWS + j + 1, :], (STEP, LANES)
                        )
                        for k in range(3)
                    ]
                    for j in range(size)
                ]
                for m in range(half, half + part, STEP):
                    lorentz_sum, gauss_sum = None, None
                    for j, (scale, lorentz, gauss) in enumerate(rows):
                        reach = squares[first + j, m : m + STEP, :] * scale - 1.0
                        one_l, one_g = lorentz / reach, gauss * jnp.exp2(reach)
                        lorentz_sum = one_l if j == 0 else lorentz_sum + one_l
                        gauss_sum = one_g if j == 0 else gauss_sum + one_g
                    high, low = split(lorentz_sum + gauss_sum, 2)
                    mixed[m : m + STEP, 2 * g * LANES : (2 * g + 1) * LANES] = high
                    mixed[m : m + STEP, (2 * g + 1) * LANES : (2 * g + 2) * LANES] = low
            tiles[t, :, half : half + part] = lax.dot_general(
                seats,
                mixed[half : half + part, :],
                (((1,), (1,)), ((), ())),
                preferred_element_type=f32,
            )
        return carry

    lax.fori_loop(0, THERMAL_SAMPLES, one, 0, unroll=4)

    high, low = split(tiles[...].reshape(depth, PATCH_SAMPLES), 2)
    coefficients = jnp.dot(
        spread[...], jnp.concatenate([high, high, low]), preferred_element_type=f32
    )
    for lot in range(plan.lots):
        for half in range(2):
            sent[pl.ds(2 * lot + half, devices, stride=plan.rows), :] = coefficients[
                lot * devices : (lot + 1) * devices, half * LANES : (half + 1) * LANES
            ]


def place_kernel(plan, got, out):
    f32 = jnp.float32
    senders = plan.lines_n * plan.temp_n
    chunks = SPAN_SAMPLES // LANES
    lane = lax.broadcasted_iota(jnp.int32, (senders, LANES), 1).astype(f32)

    def take(row):
        return got[pl.ds(row, senders, stride=plan.rows), :]

    begins = take(2 * plan.lots)
    hits, spread = [], []
    for slot in range(plan.cap):
        begin = begins[:, slot * PIECE : slot * PIECE + 1]
        chunk = jnp.floor(begin * (1.0 / LANES))
        own = jnp.floor(chunk * (1.0 / chunks))
        early = lane >= begin - chunk * LANES
        target = (chunk - own * chunks) * ROWS + own
        for order in range(plan.orders):
            lot = slot * plan.orders + order
            left, right = take(2 * lot), take(2 * lot + 1)
            hits.append(jnp.where(target + order * plan.held == lane, 1.0, 0.0))
            spread.append(
                jnp.concatenate(
                    [jnp.where(early, left, 0.0), right, jnp.where(early, 0.0, left)], axis=1
                )
            )
    landed = lax.dot_general(
        jnp.concatenate(hits).astype(jnp.bfloat16),
        jnp.concatenate(split(jnp.concatenate(spread), 3), axis=1),
        (((0,), (0,)), ((), ())),
        preferred_element_type=f32,
    )
    landed = landed[:, : 3 * LANES] + landed[:, 3 * LANES : 6 * LANES] + landed[:, 6 * LANES :]
    for c in range(chunks):
        total = landed[c * ROWS : (c + 1) * ROWS, :LANES]
        for back in (1, 2):
            if c >= back:
                total = total + landed[
                    (c - back) * ROWS : (c - back + 1) * ROWS, back * LANES : (back + 1) * LANES
                ]
        for order_at in range(plan.orders):
            out[order_at, :, c * LANES : (c + 1) * LANES] = total[
                order_at * plan.held : (order_at + 1) * plan.held
            ]


def on_device(
    line_position,
    line_strength,
    lower_energy,
    broad_width,
    broad_exponent,
    doppler_width,
    block_window,
    tile_offset,
    owner_slot,
):
    plan = Plan(
        lax.axis_size("lines"),
        lax.axis_size("temp"),
        line_position.shape[0],
        owner_slot.shape[0],
    )
    devices = plan.lines_n * plan.temp_n
    f32 = jnp.float32
    sent = pl.pallas_call(
        functools.partial(tile_kernel, plan),
        out_shape=pltpu.VMEM((devices * plan.rows, LANES), f32),
        scratch_shapes=[
            pltpu.VMEM((THERMAL_SAMPLES, 3, len(plan.groups) * ROWS, LANES), f32),
            pltpu.VMEM((plan.share, PATCH_SAMPLES, LANES), f32),
            pltpu.VMEM((PATCH_SAMPLES, 2 * LANES * len(plan.groups)), jnp.bfloat16),
            pltpu.VMEM((THERMAL_SAMPLES, SEATS, PATCH_SAMPLES), f32),
            pltpu.VMEM((plan.lots * devices, 3 * THERMAL_SAMPLES * SEATS), jnp.bfloat16),
        ],
        name="tiles",
    )(
        line_position,
        line_strength,
        lower_energy,
        broad_width,
        broad_exponent,
        doppler_width,
        block_window[None, :],
        tile_offset[None, :],
        owner_slot[None, :],
        jnp.asarray(plan.table()),
    )
    got = lax.all_to_all(
        sent.reshape(devices, 1, plan.rows * LANES), ("lines", "temp"), 0, 0, tiled=True
    )
    return pl.pallas_call(
        functools.partial(place_kernel, plan),
        out_shape=jax.ShapeDtypeStruct((plan.orders, plan.held, SPAN_SAMPLES), f32),
        name="place",
    )(pltpu.with_memory_space_constraint(got.reshape(devices * plan.rows, LANES), pltpu.VMEM))


def solution(mesh):
    return jax.shard_map(
        on_device,
        mesh=mesh,
        in_specs=(
            P("lines", None),
            P("lines", None),
            P("lines", None),
            P("lines", None),
            P("lines", None),
            P("lines", None),
            P("lines"),
            P("lines"),
            P(),
        ),
        out_specs=P("temp", "lines", None),
        check_vma=False,
    )
```

```python
import functools
import math

import jax
import jax.numpy as jnp
import numpy as np
from jax import lax
from jax.experimental import pallas as pl
from jax.experimental.pallas import tpu as pltpu
from jax.sharding import PartitionSpec as P

LANES = 128
ROWS = 8
PATCH_SAMPLES = 256
SPAN_SAMPLES = 2048
THERMAL_SAMPLES = 8
REFERENCE_KELVIN = 1000.0
PIECE = 32
SEATS = 16
GROUP = 8
STEP = 16
HIGHEST = lax.Precision.HIGHEST


def kelvins():
    theta = math.pi * (np.arange(THERMAL_SAMPLES) + 0.5) / THERMAL_SAMPLES
    return [float(k) for k in 1650.0 + 1350.0 * np.cos(theta)]


def regression():
    order = np.arange(THERMAL_SAMPLES)
    theta = math.pi * (np.arange(THERMAL_SAMPLES) + 0.5) / THERMAL_SAMPLES
    factor = np.where(order == 0, 1.0, 2.0) / THERMAL_SAMPLES
    return factor[:, None] * np.cos(order[:, None] * theta[None, :])


class Plan:
    def __init__(self, lines_n, temp_n, blocks, spans):
        self.lines_n, self.temp_n, self.blocks, self.spans = lines_n, temp_n, blocks, spans
        self.held = spans // lines_n
        self.orders = THERMAL_SAMPLES // temp_n
        self.share = -(-blocks // temp_n)
        self.groups, first = [], 0
        while first < self.share:
            size = min(GROUP, 2 ** int(math.log2(self.share - first)))
            self.groups.append((first, size))
            first += size
        heavy = 3 * ((2 * blocks) // (3 * lines_n))
        self.cap = -(-heavy // temp_n)
        self.lots = self.cap * self.orders
        self.rows = 2 * self.lots + 1
        assert self.share <= SEATS and self.cap <= LANES // PIECE and blocks % temp_n == 0
        assert self.orders * self.held <= ROWS and ROWS % temp_n == 0

    def table(self):
        weight = regression().astype(np.float32)
        rows = [
            [weight[(d % self.temp_n) * self.orders + order] for d in range(ROWS)]
            for order in range(self.orders)
        ]
        return np.repeat(np.array(rows), SEATS, axis=2)


def line_terms(strength, energy, broad, power, doppler, kelvin):
    inverse = 1.0 / kelvin
    scaled = strength * jnp.exp(energy * (1.0 / REFERENCE_KELVIN - inverse))
    lw = 2.0 * broad * jnp.exp(power * math.log(REFERENCE_KELVIN * inverse))
    gw = (2.35482 * math.sqrt(kelvin / REFERENCE_KELVIN)) * doppler
    g2, l2 = gw * gw, lw * lw
    g3, l3 = g2 * gw, l2 * lw
    g4, l4 = g2 * g2, l2 * l2
    total = (
        g4 * gw
        + 2.69269 * g4 * lw
        + 2.42843 * g3 * l2
        + 4.47163 * g2 * l3
        + 0.07842 * gw * l4
        + l4 * lw
    )
    full = jnp.exp(0.2 * jnp.log(total))
    narrow = 1.0 / full
    share = lw * narrow
    mixing = share * (1.36603 + share * (-0.47719 + share * 0.11116))
    lorentz = (-2.0 / math.pi) * narrow * scaled * mixing
    gauss = (2.0 * 0.939437) * narrow * scaled * (1.0 - mixing)
    return -4.0 * narrow * narrow, lorentz, gauss


def quotient(values, power):
    return lax.shift_right_logical(values, jnp.int32(power.bit_length() - 1))


def remainder(values, power):
    return values & (power - 1)


def split(values, parts):
    out = []
    for part in range(parts):
        out.append(values.astype(jnp.bfloat16))
        if part < parts - 1:
            values = values - out[-1].astype(jnp.float32)
    return out


def choose(ones, values, parts):
    return jnp.dot(
        jnp.concatenate([ones.astype(jnp.bfloat16)] * parts, axis=1),
        jnp.concatenate(split(values, parts)),
        preferred_element_type=jnp.float32,
    )


def tile_kernel(
    plan,
    position,
    strength,
    energy,
    broad,
    power,
    doppler,
    window,
    offset,
    owner_slot,
    table,
    sent,
    terms,
    squares,
    mixed,
    tiles,
    spread,
):
    blocks, temp_n = plan.blocks, plan.temp_n
    me = lax.axis_index("temp").astype(jnp.float32)
    f32 = jnp.float32

    def iota(shape, axis):
        return lax.broadcasted_iota(jnp.int32, shape, axis).astype(f32)

    down, across = iota((blocks, blocks), 0), iota((blocks, blocks), 1)
    eye = down == across

    def stand(row):
        return jnp.sum(jnp.where(eye, row, 0.0), axis=1, keepdims=True)

    def lay(column):
        return jnp.sum(jnp.where(eye, column, 0.0), axis=0, keepdims=True)

    window_column = stand(window[...].astype(f32))
    offset_column = stand(offset[...].astype(f32))
    seat = owner_slot[...].astype(f32)
    slot_column = jnp.sum(
        jnp.where(window_column == iota((blocks, plan.spans), 1), seat, 0.0), axis=1, keepdims=True
    )
    owner_column = jnp.floor((slot_column + 0.5) * (1.0 / plan.held))
    owner_row = lay(owner_column)
    begin_column = (slot_column - owner_column * plan.held) * SPAN_SAMPLES + offset_column
    key_column = owner_column * blocks + iota((blocks, 1), 0)
    key_row = owner_row * blocks + iota((1, blocks), 1)
    rank_row = jnp.sum(jnp.where(key_column < key_row, 1.0, 0.0), axis=0, keepdims=True)
    rank_column = jnp.sum(jnp.where(key_row < key_column, 1.0, 0.0), axis=1, keepdims=True)

    spans = [size * ROWS for _, size in plan.groups]
    starts = [sum(spans[:g]) for g in range(len(spans))]
    pick_row = lax.broadcasted_iota(jnp.int32, (sum(spans), blocks), 0)
    local = jnp.zeros((sum(spans), blocks), jnp.int32)
    for (first, size), start in zip(plan.groups, starts):
        turned = pick_row - start
        turned = first + remainder(quotient(turned, ROWS) + turned, size)
        local = jnp.where(pick_row >= start, turned, local)
    pick = jnp.where(rank_row == (local * temp_n).astype(f32) + me, 1.0, 0.0)

    def gather(values):
        return choose(pick, values, 3)

    row = lax.broadcasted_iota(jnp.int32, (ROWS, LANES), 0)
    lane = lax.broadcasted_iota(jnp.int32, (ROWS, LANES), 1)

    def pack(values):
        out = []
        for (_, size), start in zip(plan.groups, starts):
            width = LANES // size
            part = values[start : start + ROWS]
            for turn in range(1, size):
                turned = values[start + turn * ROWS : start + (turn + 1) * ROWS]
                part = jnp.where(quotient(lane, width) == turn, turned, part)
            if size == ROWS:
                part = pltpu.roll(part, 0, 1, stride=width, stride_axis=0)
            else:
                for bit in range(size.bit_length() - 1):
                    step = 1 << bit
                    turned = pltpu.roll(part, step * width, 1)
                    part = jnp.where(row & step != 0, turned, part)
            out.append(part)
        return out

    begin = gather(jnp.broadcast_to(begin_column, (blocks, LANES)))
    every = [r[...] for r in (position, strength, energy, broad, power, doppler)]
    every = gather(jnp.concatenate(every, axis=1))
    columns = [pack(every[:, i * LANES : (i + 1) * LANES]) for i in range(6)]
    begin_packed = pack(begin)
    for g in range(len(plan.groups)):
        for t, kelvin in enumerate(kelvins()):
            for k, value in enumerate(line_terms(*(c[g] for c in columns[1:]), kelvin)):
                terms[t, k, g * ROWS : (g + 1) * ROWS] = value

    depth = THERMAL_SAMPLES * SEATS
    column = remainder(lax.broadcasted_iota(jnp.int32, (blocks, depth), 1), SEATS)
    mine = rank_column == (column * temp_n).astype(f32) + me
    real = column < plan.share
    owner_wide = jnp.sum(jnp.where(mine & real, owner_column, 0.0), axis=0, keepdims=True)
    first_wide = jnp.sum(
        jnp.where(owner_column < owner_wide, 1.0, 0.0), axis=0, keepdims=True
    )
    column_row = remainder(lax.broadcasted_iota(jnp.int32, (1, depth), 1), SEATS)
    skipped = jnp.floor((first_wide - me + (temp_n - 0.5)) * (1.0 / temp_n))
    place_wide = owner_wide * plan.cap + column_row.astype(f32) - skipped
    place_wide = jnp.where(column_row < plan.share, place_wide, -2.0)

    begins = jnp.concatenate(
        [begin[start : start + size] for (_, size), start in zip(plan.groups, starts)]
        + [jnp.zeros((SEATS - plan.share, LANES), f32)] * (SEATS > plan.share)
    )
    devices = plan.lines_n * temp_n
    receiver = lax.broadcasted_iota(jnp.int32, (devices, depth), 0)
    owner_place = (quotient(receiver, temp_n) * plan.cap).astype(f32)
    placed = [owner_place + slot == place_wide for slot in range(plan.cap)]
    for slot in range(plan.cap):
        for order in range(plan.orders):
            weight = jnp.concatenate([table[order]] * (devices // ROWS))
            lot = slot * plan.orders + order
            high, low = split(jnp.where(placed[slot], weight, 0.0), 2)
            spread[lot * devices : (lot + 1) * devices, :] = jnp.concatenate(
                [high, low, high], axis=1
            )
    held_lane = quotient(lax.broadcasted_iota(jnp.int32, (SEATS, LANES), 1), PIECE)
    sent[pl.ds(2 * plan.lots, devices, stride=plan.rows), :] = choose(
        jnp.concatenate([jnp.where(p[:, :SEATS], 1.0, 0.0) for p in placed], axis=1),
        jnp.concatenate(
            [jnp.where(held_lane == slot, begins, 0.0) for slot in range(plan.cap)]
        ),
        2,
    )

    grid = iota((PATCH_SAMPLES, LANES), 0)
    for g, (first, size) in enumerate(plan.groups):
        start = begin_packed[g][:1]
        point = grid - (start - jnp.floor(start * (1.0 / LANES)) * LANES)
        point = jnp.where(point < 0.0, point + PATCH_SAMPLES, point) + 0.5
        for j in range(size):
            distance = point - columns[0][g][j : j + 1]
            squares[first + j] = distance * distance

    width = 2 * LANES * len(plan.groups)
    held_by = lax.broadcasted_iota(jnp.int32, (SEATS, width), 1)
    seat_of = jnp.zeros((SEATS, width), jnp.int32)
    for g, (first, size) in enumerate(plan.groups):
        seat = first + quotient(remainder(held_by, LANES), LANES // size)
        seat_of = jnp.where(quotient(held_by, 2 * LANES) == g, seat, seat_of)
    seats = jnp.where(
        seat_of == lax.broadcasted_iota(jnp.int32, (SEATS, width), 0), 1.0, 0.0
    ).astype(jnp.bfloat16)

    def one(t, carry):
        part = PATCH_SAMPLES // 2
        for half in range(0, PATCH_SAMPLES, part):
            for g, (first, size) in enumerate(plan.groups):
                rows = [
                    [
                        jnp.broadcast_to(
                            terms[t, k, g * ROWS + j : g * ROWS + j + 1, :], (STEP, LANES)
                        )
                        for k in range(3)
                    ]
                    for j in range(size)
                ]
                for m in range(half, half + part, STEP):
                    lorentz_sum, gauss_sum = None, None
                    for j, (scale, lorentz, gauss) in enumerate(rows):
                        reach = squares[first + j, m : m + STEP, :] * scale - 1.0
                        one_l, one_g = lorentz / reach, gauss * jnp.exp2(reach)
                        lorentz_sum = one_l if j == 0 else lorentz_sum + one_l
                        gauss_sum = one_g if j == 0 else gauss_sum + one_g
                    high, low = split(lorentz_sum + gauss_sum, 2)
                    mixed[m : m + STEP, 2 * g * LANES : (2 * g + 1) * LANES] = high
                    mixed[m : m + STEP, (2 * g + 1) * LANES : (2 * g + 2) * LANES] = low
            tiles[t, :, half : half + part] = lax.dot_general(
                seats,
                mixed[half : half + part, :],
                (((1,), (1,)), ((), ())),
                preferred_element_type=f32,
            )
        return carry

    lax.fori_loop(0, THERMAL_SAMPLES, one, 0, unroll=4)

    high, low = split(tiles[...].reshape(depth, PATCH_SAMPLES), 2)
    coefficients = jnp.dot(
        spread[...], jnp.concatenate([high, high, low]), preferred_element_type=f32
    )
    for lot in range(plan.lots):
        for half in range(2):
            sent[pl.ds(2 * lot + half, devices, stride=plan.rows), :] = coefficients[
                lot * devices : (lot + 1) * devices, half * LANES : (half + 1) * LANES
            ]


def place_kernel(plan, got, out):
    f32 = jnp.float32
    senders = plan.lines_n * plan.temp_n
    chunks = SPAN_SAMPLES // LANES
    lane = lax.broadcasted_iota(jnp.int32, (senders, LANES), 1).astype(f32)

    def take(row):
        return got[pl.ds(row, senders, stride=plan.rows), :]

    begins = take(2 * plan.lots)
    hits, spread = [], []
    for slot in range(plan.cap):
        begin = begins[:, slot * PIECE : slot * PIECE + 1]
        chunk = jnp.floor(begin * (1.0 / LANES))
        own = jnp.floor(chunk * (1.0 / chunks))
        early = lane >= begin - chunk * LANES
        target = (chunk - own * chunks) * ROWS + own
        for order in range(plan.orders):
            lot = slot * plan.orders + order
            left, right = take(2 * lot), take(2 * lot + 1)
            hits.append(jnp.where(target + order * plan.held == lane, 1.0, 0.0))
            spread.append(
                jnp.concatenate(
                    [jnp.where(early, left, 0.0), right, jnp.where(early, 0.0, left)], axis=1
                )
            )
    landed = lax.dot_general(
        jnp.concatenate(hits).astype(jnp.bfloat16),
        jnp.concatenate(split(jnp.concatenate(spread), 3), axis=1),
        (((0,), (0,)), ((), ())),
        preferred_element_type=f32,
    )
    landed = landed[:, : 3 * LANES] + landed[:, 3 * LANES : 6 * LANES] + landed[:, 6 * LANES :]
    for c in range(chunks):
        total = landed[c * ROWS : (c + 1) * ROWS, :LANES]
        for back in (1, 2):
            if c >= back:
                total = total + landed[
                    (c - back) * ROWS : (c - back + 1) * ROWS, back * LANES : (back + 1) * LANES
                ]
        for order_at in range(plan.orders):
            out[order_at, :, c * LANES : (c + 1) * LANES] = total[
                order_at * plan.held : (order_at + 1) * plan.held
            ]


def on_device(
    line_position,
    line_strength,
    lower_energy,
    broad_width,
    broad_exponent,
    doppler_width,
    block_window,
    tile_offset,
    owner_slot,
):
    plan = Plan(
        lax.axis_size("lines"),
        lax.axis_size("temp"),
        line_position.shape[0],
        owner_slot.shape[0],
    )
    devices = plan.lines_n * plan.temp_n
    f32 = jnp.float32
    sent = pl.pallas_call(
        functools.partial(tile_kernel, plan),
        out_shape=pltpu.VMEM((devices * plan.rows, LANES), f32),
        scratch_shapes=[
            pltpu.VMEM((THERMAL_SAMPLES, 3, len(plan.groups) * ROWS, LANES), f32),
            pltpu.VMEM((plan.share, PATCH_SAMPLES, LANES), f32),
            pltpu.VMEM((PATCH_SAMPLES, 2 * LANES * len(plan.groups)), jnp.bfloat16),
            pltpu.VMEM((THERMAL_SAMPLES, SEATS, PATCH_SAMPLES), f32),
            pltpu.VMEM((plan.lots * devices, 3 * THERMAL_SAMPLES * SEATS), jnp.bfloat16),
        ],
        name="tiles",
    )(
        line_position,
        line_strength,
        lower_energy,
        broad_width,
        broad_exponent,
        doppler_width,
        block_window[None, :],
        tile_offset[None, :],
        owner_slot[None, :],
        jnp.asarray(plan.table()),
    )
    got = lax.all_to_all(
        sent.reshape(devices, 1, plan.rows * LANES), ("lines", "temp"), 0, 0, tiled=True
    )
    return pl.pallas_call(
        functools.partial(place_kernel, plan),
        out_shape=jax.ShapeDtypeStruct((plan.orders, plan.held, SPAN_SAMPLES), f32),
        name="place",
    )(pltpu.with_memory_space_constraint(got.reshape(devices * plan.rows, LANES), pltpu.VMEM))


def solution(mesh):
    return jax.shard_map(
        on_device,
        mesh=mesh,
        in_specs=(
            P("lines", None),
            P("lines", None),
            P("lines", None),
            P("lines", None),
            P("lines", None),
            P("lines", None),
            P("lines"),
            P("lines"),
            P(),
        ),
        out_specs=P("temp", "lines", None),
        check_vma=False,
    )
```

```python
import functools
import math

import jax
import jax.numpy as jnp
import numpy as np
from jax import lax
from jax.experimental import pallas as pl
from jax.experimental.pallas import tpu as pltpu
from jax.sharding import PartitionSpec as P

LANES = 128
ROWS = 8
PATCH_SAMPLES = 256
SPAN_SAMPLES = 2048
THERMAL_SAMPLES = 8
REFERENCE_KELVIN = 1000.0
PIECE = 32
SEATS = 16
GROUP = 8
STEP = 16


def kelvins():
    theta = math.pi * (np.arange(THERMAL_SAMPLES) + 0.5) / THERMAL_SAMPLES
    return [float(k) for k in 1650.0 + 1350.0 * np.cos(theta)]


def regression():
    order = np.arange(THERMAL_SAMPLES)
    theta = math.pi * (np.arange(THERMAL_SAMPLES) + 0.5) / THERMAL_SAMPLES
    factor = np.where(order == 0, 1.0, 2.0) / THERMAL_SAMPLES
    return factor[:, None] * np.cos(order[:, None] * theta[None, :])


class Plan:
    def __init__(self, lines_n, temp_n, blocks, spans):
        self.lines_n, self.temp_n, self.blocks, self.spans = lines_n, temp_n, blocks, spans
        self.held = spans // lines_n
        self.orders = THERMAL_SAMPLES // temp_n
        self.share = -(-blocks // temp_n)
        self.groups, first = [], 0
        while first < self.share:
            size = min(GROUP, 2 ** int(math.log2(self.share - first)))
            self.groups.append((first, size))
            first += size
        heavy = 3 * ((2 * blocks) // (3 * lines_n))
        self.cap = -(-heavy // temp_n)
        self.lots = self.cap * self.orders
        self.rows = 2 * self.lots + 1
        assert self.share <= SEATS and self.cap <= LANES // PIECE and blocks % temp_n == 0
        assert self.orders * self.held <= ROWS and ROWS % temp_n == 0

    def table(self):
        weight = regression().astype(np.float32)
        rows = [
            [weight[(d % self.temp_n) * self.orders + order] for d in range(ROWS)]
            for order in range(self.orders)
        ]
        return np.repeat(np.array(rows), SEATS, axis=2)


def line_terms(strength, energy, broad, power, doppler, kelvin):
    inverse = 1.0 / kelvin
    scaled = strength * jnp.exp(energy * (1.0 / REFERENCE_KELVIN - inverse))
    lw = 2.0 * broad * jnp.exp(power * math.log(REFERENCE_KELVIN * inverse))
    gw = (2.35482 * math.sqrt(kelvin / REFERENCE_KELVIN)) * doppler
    g2, l2 = gw * gw, lw * lw
    g3, l3 = g2 * gw, l2 * lw
    g4, l4 = g2 * g2, l2 * l2
    total = (
        g4 * gw
        + 2.69269 * g4 * lw
        + 2.42843 * g3 * l2
        + 4.47163 * g2 * l3
        + 0.07842 * gw * l4
        + l4 * lw
    )
    full = jnp.exp(0.2 * jnp.log(total))
    narrow = 1.0 / full
    share = lw * narrow
    mixing = share * (1.36603 + share * (-0.47719 + share * 0.11116))
    lorentz = (-2.0 / math.pi) * narrow * scaled * mixing
    gauss = (2.0 * 0.939437) * narrow * scaled * (1.0 - mixing)
    return -4.0 * narrow * narrow, lorentz, gauss


def quotient(values, power):
    return lax.shift_right_logical(values, jnp.int32(power.bit_length() - 1))


def remainder(values, power):
    return values & (power - 1)


def split(values, parts):
    out = []
    for part in range(parts):
        out.append(values.astype(jnp.bfloat16))
        if part < parts - 1:
            values = values - out[-1].astype(jnp.float32)
    return out


def choose(ones, values, parts):
    return jnp.dot(
        jnp.concatenate([ones.astype(jnp.bfloat16)] * parts, axis=1),
        jnp.concatenate(split(values, parts)),
        preferred_element_type=jnp.float32,
    )


def tile_kernel(
    plan,
    position,
    strength,
    energy,
    broad,
    power,
    doppler,
    window,
    offset,
    owner_slot,
    table,
    sent,
    terms,
    squares,
    mixed,
    tiles,
    spread,
):
    blocks, temp_n = plan.blocks, plan.temp_n
    me = lax.axis_index("temp").astype(jnp.float32)
    f32 = jnp.float32

    def iota(shape, axis):
        return lax.broadcasted_iota(jnp.int32, shape, axis).astype(f32)

    eye = iota((blocks, blocks), 0) == iota((blocks, blocks), 1)

    def stand(row):
        return jnp.sum(jnp.where(eye, row, 0.0), axis=1, keepdims=True)

    def lay(column):
        return jnp.sum(jnp.where(eye, column, 0.0), axis=0, keepdims=True)

    window_column = stand(window[...].astype(f32))
    offset_column = stand(offset[...].astype(f32))
    seat = owner_slot[...].astype(f32)
    slot_column = jnp.sum(
        jnp.where(window_column == iota((blocks, plan.spans), 1), seat, 0.0), axis=1, keepdims=True
    )
    owner_column = jnp.floor((slot_column + 0.5) * (1.0 / plan.held))
    owner_row = lay(owner_column)
    begin_column = (slot_column - owner_column * plan.held) * SPAN_SAMPLES + offset_column
    key_column = owner_column * blocks + iota((blocks, 1), 0)
    key_row = owner_row * blocks + iota((1, blocks), 1)
    rank_row = jnp.sum(jnp.where(key_column < key_row, 1.0, 0.0), axis=0, keepdims=True)
    rank_column = jnp.sum(jnp.where(key_row < key_column, 1.0, 0.0), axis=1, keepdims=True)

    spans = [size * ROWS for _, size in plan.groups]
    starts = [sum(spans[:g]) for g in range(len(spans))]
    pick_row = lax.broadcasted_iota(jnp.int32, (sum(spans), blocks), 0)
    local = jnp.zeros((sum(spans), blocks), jnp.int32)
    for (first, size), start in zip(plan.groups, starts):
        turned = pick_row - start
        turned = first + remainder(quotient(turned, ROWS) + turned, size)
        local = jnp.where(pick_row >= start, turned, local)
    pick = jnp.where(rank_row == (local * temp_n).astype(f32) + me, 1.0, 0.0)

    def gather(values):
        return choose(pick, values, 3)

    row = lax.broadcasted_iota(jnp.int32, (ROWS, LANES), 0)
    lane = lax.broadcasted_iota(jnp.int32, (ROWS, LANES), 1)

    def pack(values):
        out = []
        for (_, size), start in zip(plan.groups, starts):
            width = LANES // size
            part = values[start : start + ROWS]
            for turn in range(1, size):
                turned = values[start + turn * ROWS : start + (turn + 1) * ROWS]
                part = jnp.where(quotient(lane, width) == turn, turned, part)
            if size == ROWS:
                part = pltpu.roll(part, 0, 1, stride=width, stride_axis=0)
            else:
                for bit in range(size.bit_length() - 1):
                    step = 1 << bit
                    turned = pltpu.roll(part, step * width, 1)
                    part = jnp.where(row & step != 0, turned, part)
            out.append(part)
        return out

    begin = gather(jnp.broadcast_to(begin_column, (blocks, LANES)))
    every = [r[...] for r in (position, strength, energy, broad, power, doppler)]
    every = gather(jnp.concatenate(every, axis=1))
    columns = [pack(every[:, i * LANES : (i + 1) * LANES]) for i in range(6)]
    begin_packed = pack(begin)
    for g in range(len(plan.groups)):
        for t, kelvin in enumerate(kelvins()):
            for k, value in enumerate(line_terms(*(c[g] for c in columns[1:]), kelvin)):
                terms[t, k, g * ROWS : (g + 1) * ROWS] = value

    depth = THERMAL_SAMPLES * SEATS
    column = remainder(lax.broadcasted_iota(jnp.int32, (blocks, depth), 1), SEATS)
    mine = rank_column == (column * temp_n).astype(f32) + me
    real = column < plan.share
    owner_wide = jnp.sum(jnp.where(mine & real, owner_column, 0.0), axis=0, keepdims=True)
    first_wide = jnp.sum(
        jnp.where(owner_column < owner_wide, 1.0, 0.0), axis=0, keepdims=True
    )
    column_row = remainder(lax.broadcasted_iota(jnp.int32, (1, depth), 1), SEATS)
    skipped = jnp.floor((first_wide - me + (temp_n - 0.5)) * (1.0 / temp_n))
    place_wide = owner_wide * plan.cap + column_row.astype(f32) - skipped
    place_wide = jnp.where(column_row < plan.share, place_wide, -2.0)

    begins = jnp.concatenate(
        [begin[start : start + size] for (_, size), start in zip(plan.groups, starts)]
        + [jnp.zeros((SEATS - plan.share, LANES), f32)] * (SEATS > plan.share)
    )
    devices = plan.lines_n * temp_n
    receiver = lax.broadcasted_iota(jnp.int32, (devices, depth), 0)
    owner_place = (quotient(receiver, temp_n) * plan.cap).astype(f32)
    placed = [owner_place + slot == place_wide for slot in range(plan.cap)]
    for slot in range(plan.cap):
        for order in range(plan.orders):
            weight = jnp.concatenate([table[order]] * (devices // ROWS))
            lot = slot * plan.orders + order
            high, low = split(jnp.where(placed[slot], weight, 0.0), 2)
            spread[lot * devices : (lot + 1) * devices, :] = jnp.concatenate(
                [high, low, high], axis=1
            )
    held_lane = quotient(lax.broadcasted_iota(jnp.int32, (SEATS, LANES), 1), PIECE)
    sent[pl.ds(2 * plan.lots, devices, stride=plan.rows), :] = choose(
        jnp.concatenate([jnp.where(p[:, :SEATS], 1.0, 0.0) for p in placed], axis=1),
        jnp.concatenate(
            [jnp.where(held_lane == slot, begins, 0.0) for slot in range(plan.cap)]
        ),
        2,
    )

    grid = iota((PATCH_SAMPLES, LANES), 0)
    for g, (first, size) in enumerate(plan.groups):
        start = begin_packed[g][:1]
        point = grid - (start - jnp.floor(start * (1.0 / LANES)) * LANES)
        point = jnp.where(point < 0.0, point + PATCH_SAMPLES, point) + 0.5
        for j in range(size):
            distance = point - columns[0][g][j : j + 1]
            squares[first + j] = distance * distance

    width = 2 * LANES * len(plan.groups)
    held_by = lax.broadcasted_iota(jnp.int32, (SEATS, width), 1)
    seat_of = jnp.zeros((SEATS, width), jnp.int32)
    for g, (first, size) in enumerate(plan.groups):
        seat = first + quotient(remainder(held_by, LANES), LANES // size)
        seat_of = jnp.where(quotient(held_by, 2 * LANES) == g, seat, seat_of)
    seats = jnp.where(
        seat_of == lax.broadcasted_iota(jnp.int32, (SEATS, width), 0), 1.0, 0.0
    ).astype(jnp.bfloat16)

    def one(t, carry):
        part = PATCH_SAMPLES // 2
        for half in range(0, PATCH_SAMPLES, part):
            for g, (first, size) in enumerate(plan.groups):
                rows = [
                    [
                        jnp.broadcast_to(
                            terms[t, k, g * ROWS + j : g * ROWS + j + 1, :], (ROWS, LANES)
                        )
                        for k in range(3)
                    ]
                    for j in range(size)
                ]
                for m in range(half, half + part, STEP):
                    sums = []
                    for at in range(m, m + STEP, ROWS):
                        total = None
                        for j, (scale, lorentz, gauss) in enumerate(rows):
                            reach = squares[first + j, at : at + ROWS, :] * scale - 1.0
                            term = lorentz / reach + gauss * jnp.exp2(reach)
                            total = term if j == 0 else total + term
                        sums.append(total)
                    high, low = split(jnp.concatenate(sums), 2)
                    mixed[m : m + STEP, 2 * g * LANES : (2 * g + 1) * LANES] = high
                    mixed[m : m + STEP, (2 * g + 1) * LANES : (2 * g + 2) * LANES] = low
            tiles[t, :, half : half + part] = lax.dot_general(
                seats,
                mixed[half : half + part, :],
                (((1,), (1,)), ((), ())),
                preferred_element_type=f32,
            )
        return carry

    lax.fori_loop(0, THERMAL_SAMPLES, one, 0, unroll=4)

    high, low = split(tiles[...].reshape(depth, PATCH_SAMPLES), 2)
    coefficients = jnp.dot(
        spread[...], jnp.concatenate([high, high, low]), preferred_element_type=f32
    )
    for lot in range(plan.lots):
        for half in range(2):
            sent[pl.ds(2 * lot + half, devices, stride=plan.rows), :] = coefficients[
                lot * devices : (lot + 1) * devices, half * LANES : (half + 1) * LANES
            ]


def place_kernel(plan, got, out):
    f32 = jnp.float32
    senders = plan.lines_n * plan.temp_n
    chunks = SPAN_SAMPLES // LANES
    lane = lax.broadcasted_iota(jnp.int32, (senders, LANES), 1).astype(f32)

    def take(row):
        return got[pl.ds(row, senders, stride=plan.rows), :]

    begins = take(2 * plan.lots)
    hits, spread = [], []
    for slot in range(plan.cap):
        begin = begins[:, slot * PIECE : slot * PIECE + 1]
        chunk = jnp.floor(begin * (1.0 / LANES))
        own = jnp.floor(chunk * (1.0 / chunks))
        early = lane >= begin - chunk * LANES
        target = (chunk - own * chunks) * ROWS + own
        for order in range(plan.orders):
            lot = slot * plan.orders + order
            left, right = take(2 * lot), take(2 * lot + 1)
            hits.append(jnp.where(target + order * plan.held == lane, 1.0, 0.0))
            spread.append(
                jnp.concatenate(
                    [jnp.where(early, left, 0.0), right, jnp.where(early, 0.0, left)], axis=1
                )
            )
    landed = jnp.dot(
        jnp.transpose(jnp.concatenate(hits)).astype(jnp.bfloat16),
        jnp.concatenate(split(jnp.concatenate(spread), 2), axis=1),
        preferred_element_type=f32,
    )
    landed = landed[:, : 3 * LANES] + landed[:, 3 * LANES :]
    for c in range(chunks):
        total = landed[c * ROWS : (c + 1) * ROWS, :LANES]
        for back in (1, 2):
            if c >= back:
                total = total + landed[
                    (c - back) * ROWS : (c - back + 1) * ROWS, back * LANES : (back + 1) * LANES
                ]
        for order_at in range(plan.orders):
            out[order_at, :, c * LANES : (c + 1) * LANES] = total[
                order_at * plan.held : (order_at + 1) * plan.held
            ]


def on_device(
    line_position,
    line_strength,
    lower_energy,
    broad_width,
    broad_exponent,
    doppler_width,
    block_window,
    tile_offset,
    owner_slot,
):
    plan = Plan(
        lax.axis_size("lines"),
        lax.axis_size("temp"),
        line_position.shape[0],
        owner_slot.shape[0],
    )
    devices = plan.lines_n * plan.temp_n
    f32 = jnp.float32
    sent = pl.pallas_call(
        functools.partial(tile_kernel, plan),
        out_shape=pltpu.VMEM((devices * plan.rows, LANES), f32),
        scratch_shapes=[
            pltpu.VMEM((THERMAL_SAMPLES, 3, len(plan.groups) * ROWS, LANES), f32),
            pltpu.VMEM((plan.share, PATCH_SAMPLES, LANES), f32),
            pltpu.VMEM((PATCH_SAMPLES, 2 * LANES * len(plan.groups)), jnp.bfloat16),
            pltpu.VMEM((THERMAL_SAMPLES, SEATS, PATCH_SAMPLES), f32),
            pltpu.VMEM((plan.lots * devices, 3 * THERMAL_SAMPLES * SEATS), jnp.bfloat16),
        ],
        name="tiles",
    )(
        line_position,
        line_strength,
        lower_energy,
        broad_width,
        broad_exponent,
        doppler_width,
        block_window[None, :],
        tile_offset[None, :],
        owner_slot[None, :],
        jnp.asarray(plan.table()),
    )
    got = lax.all_to_all(
        sent.reshape(devices, 1, plan.rows * LANES), ("lines", "temp"), 0, 0, tiled=True
    )
    return pl.pallas_call(
        functools.partial(place_kernel, plan),
        out_shape=jax.ShapeDtypeStruct((plan.orders, plan.held, SPAN_SAMPLES), f32),
        name="place",
    )(pltpu.with_memory_space_constraint(got.reshape(devices * plan.rows, LANES), pltpu.VMEM))


def solution(mesh):
    return jax.shard_map(
        on_device,
        mesh=mesh,
        in_specs=(
            P("lines", None),
            P("lines", None),
            P("lines", None),
            P("lines", None),
            P("lines", None),
            P("lines", None),
            P("lines"),
            P("lines"),
            P(),
        ),
        out_specs=P("temp", "lines", None),
        check_vma=False,
    )
```
